128 devices in a mesh: dp: 8 (over x, core), blk: 16 (over z, y).
Axes of the slice: x: 4, y: 4, z: 4, core: 2. Of those that a mesh axis runs over, the one named last changes fastest.
Arguments:
- rows: bfloat16 [131072, 768], P(('dp', 'blk')), may hold values from -6 to 6
- block_ids: int32 [131072, 1], P(('dp', 'blk')), may hold values from 0 to 127; in each aligned block of 1024 rows (0 to 1023, 1024 to 2047, ...) at most 16 rows name the same one
- centroids: float32 [131072, 768], P(('dp', 'blk')), may hold values from -6 to 6
- pairing: int32 [2], replicated, may hold values from 1 to 15
Outputs:
- centers: float32 [131072, 768], P(('dp', 'blk'))
- energy: float32 [131072], P(('dp', 'blk'))
The draws below stay inside these ranges and needn't reach their ends.
Inputs may be any that keep to these rules, and one draw needn't show every extreme that they name: Row r belongs to the block owned by the device of flat index block_ids[r, 0] over dp+blk with dp slowest; among the rows of one device no id occurs more than 16 times, and that many is reached in every draw. In pass p, the blocks at positions k and k XOR pairing[p] of one group are partners.
All inputs are finite; a program needn't handle non-finite values.
Results may differ from the reference program's by a relative error of at most 0.007.
Values may be sent and summed in bfloat16 or wider, within the bound.
No kernel may reach another device: no remote copies, remote signals or barrier semaphores. Data moves between devices by JAX's collectives and lax.ppermute only.
A program may use at most 64 MiB of HBM per device.

```python
import math
import jax
import jax.numpy as jnp
import numpy as np
from jax import lax

D = 768
C_DEV = 1024
ROWS_DEV = 1024
PASSES = 2
BLOCKS_GROUP = 16
CAP = 16
SLOTS = 2048
ROWS = 131072
CENTROIDS = 131072
N_DP = 8
N_BLK = 16
DEVICES = 128


def steps_of(stream_key, dims, shards, least, high):
    loudness, own = 1.0, jax.random.fold_in(stream_key, 6)
    for axis_at, blocks in shards:
        heights = jnp.exp(jax.random.uniform(jax.random.fold_in(own, axis_at), (blocks,), jnp.float32, least / len(shards), high / len(shards)))
        loudness = loudness * jnp.repeat(heights, dims[axis_at] // blocks).reshape([-1 if axis == axis_at else 1 for axis in range(len(dims))])
    return loudness


def deal_out(stream_key, own, number, rows, number_of, top, bound, slope):
    sequence = jax.random.permutation(stream_key, number_of)
    heavy_load, ordinary = portions_of(number_of, rows * top, bound, slope, True), portions_of(number_of, rows * top, bound, slope, False)
    places = jnp.arange(number_of)

    def named(sizes, turn):
        used = int((sizes > 0).sum())
        fixed = max(1, used // 4)
        shifted = fixed + (places - fixed + turn * (used - fixed)) % max(1, number_of - fixed)
        return jnp.zeros((number_of,), jnp.int32).at[sequence[jnp.where(places < fixed, places, shifted)]].set(jnp.asarray(sizes, jnp.int32))

    sizes = jnp.where(number % 4 == 0, named(heavy_load, number // 4), named(ordinary, number - number // 4 - 1))
    mixed = jax.random.permutation(jax.random.fold_in(own, 3), number_of)
    source_of, receiver = mixed[0:number_of // 2 * 2:2], mixed[1:number_of // 2 * 2:2]
    margin = jnp.minimum(sizes[source_of] - 1, bound - sizes[receiver]) // 2
    margin = jnp.where((source_of == sequence[0]) | (receiver == sequence[0]) | (sizes[receiver] == 0), 0, jnp.maximum(margin, 0))
    shifted = jax.random.randint(jax.random.fold_in(own, 4), (number_of // 2,), 0, 1 << 20) % (margin + 1)
    sizes = sizes.at[source_of].add(-shifted).at[receiver].add(shifted)
    items = jnp.searchsorted(jnp.cumsum(sizes), jnp.arange(rows * top), side="right").astype(jnp.int32)
    listing = items.reshape(top, rows).T
    listing = listing[jax.random.permutation(jax.random.fold_in(own, 1), rows)]
    turn = jax.random.randint(jax.random.fold_in(own, 2), (rows, 1), 0, top)
    return jnp.take_along_axis(listing, (jnp.arange(top)[None, :] + turn) % top, axis=1)


def portions_of(amount, total, most, slope, full):
    loads = [(1 << 20) // math.isqrt(rank ** slope) + 1 for rank in range(1, amount + 1)]
    largest = most if full else min(most, max(-(-total // amount), total * loads[0] // sum(loads)))
    least = 1 if total - largest >= amount - 1 else 0
    given, rest = [largest] + [least] * (amount - 1), total - largest - least * (amount - 1)
    while rest > 0:
        candidates = [i for i in range(1, amount) if given[i] < largest] or [i for i in range(1, amount) if given[i] < most]
        mass, remaining = sum([loads[i] for i in candidates]), rest
        for i in candidates:
            addition = min(most - given[i], max(1, remaining * loads[i] // mass), rest)
            given[i] = given[i] + addition
            rest = rest - addition
    return np.array(given)


def centred(own_key, shape, width, most, shards=(), kind=jnp.bfloat16):
    entries = width * jax.random.normal(own_key, shape, jnp.float32)
    if shards:
        entries = entries * steps_of(own_key, shape, shards, -0.22, 0.18)
    return jnp.clip(entries, -most, most).astype(kind)


def setup_inputs(seed: int = 0) -> dict:
    key_of = jax.random.split(jax.random.key(seed), 5)
    rows = centred(key_of[0], (ROWS, D), 1.0, 6.0, ((0, 128),))
    block_ids_keys = jax.random.split(jax.random.fold_in(key_of[1], 1), ROWS // ROWS_DEV)
    block_ids_turns = jax.random.permutation(jax.random.fold_in(key_of[1], 3), ROWS // ROWS_DEV)
    block_ids = jax.vmap(lambda own, number: deal_out(jax.random.fold_in(key_of[1], 2), own, number, ROWS_DEV, DEVICES, 1, CAP, 1))(block_ids_keys, block_ids_turns).reshape((ROWS, 1))
    centroids = centred(key_of[2], (CENTROIDS, D), 1.0, 6.0, ((0, 128),), jnp.float32)
    pairing = jax.random.randint(key_of[3], (PASSES,), 1, N_BLK).astype(jnp.int32)
    return {"rows": rows, "block_ids": block_ids, "centroids": centroids, "pairing": pairing}


KAPPA = 64.0

def unit_vectors(values):
    wide = values.astype(jnp.float32)
    scale = lax.rsqrt(lax.optimization_barrier(jnp.mean(wide * wide, axis=-1, keepdims=True)) + 1e-06) * values.shape[-1] ** (-0.5)
    return (wide * scale).astype(jnp.bfloat16)

def reference(rows, block_ids, centroids, pairing):
    devices = N_DP * N_BLK
    owners = block_ids[:, 0].astype(jnp.int32)
    source = jnp.arange(ROWS, dtype=jnp.int32) // ROWS_DEV
    indicator = (owners[:, None] == jnp.arange(devices, dtype=jnp.int32)[None, :]).astype(jnp.int32)
    grouped = indicator.reshape(devices, ROWS_DEV, devices)
    earlier = (jnp.cumsum(grouped, axis=1, dtype=jnp.int32) - grouped).reshape(ROWS, devices)
    position = (source * CAP + lax.optimization_barrier(jnp.sum(earlier * indicator, axis=1, dtype=jnp.int32))).astype(jnp.int32)
    unit_rows = unit_vectors(rows)
    slot_rows = jnp.zeros((devices, SLOTS, D), jnp.bfloat16).at[owners, position].set(unit_rows)
    present = jnp.zeros((devices, SLOTS), jnp.float32).at[owners, position].set(1.0)
    blocks = jnp.arange(devices, dtype=jnp.int32)
    group_base = blocks // BLOCKS_GROUP * BLOCKS_GROUP
    inside = blocks % BLOCKS_GROUP
    tiles = centroids.reshape(devices, C_DEV, D).astype(jnp.float32)
    last_totals = jnp.zeros((devices, SLOTS), jnp.float32)
    for pass_index in range(PASSES):
        unit_tiles = unit_vectors(tiles)
        partner = (group_base + jnp.bitwise_xor(inside, pairing[pass_index])).astype(jnp.int32)

        def one_block(block):
            slot_block = slot_rows[block]
            marks = present[block]
            stacked = jnp.concatenate([unit_tiles[block], unit_tiles[partner[block]]], axis=0)
            affinity = jnp.exp(KAPPA * jnp.dot(slot_block, stacked.T, preferred_element_type=jnp.float32)) * marks[:, None]
            totals = lax.optimization_barrier(jnp.sum(affinity, axis=1))
            weights = (affinity / (totals + 1.0 - marks)[:, None]).astype(jnp.bfloat16)
            sums = jnp.dot(weights.T, slot_block, preferred_element_type=jnp.float32)
            column_sums = lax.optimization_barrier(jnp.sum(weights.astype(jnp.float32), axis=0))
            return (sums[:C_DEV], sums[C_DEV:].astype(jnp.bfloat16), column_sums[:C_DEV], column_sums[C_DEV:].astype(jnp.bfloat16), totals)
        own_sums, part_sums, own_counts, part_counts, totals = lax.map(one_block, blocks)
        part_sums = lax.optimization_barrier(part_sums)
        part_counts = lax.optimization_barrier(part_counts)
        numerator = own_sums + part_sums[partner].astype(jnp.float32)
        counts = own_counts + part_counts[partner].astype(jnp.float32)
        tiles = D ** 0.5 * (numerator + unit_tiles.astype(jnp.float32)) / (counts + 1.0)[:, :, None]
        last_totals = totals
    energy = jnp.log(last_totals[owners, position] / (2.0 * C_DEV))
    return (tiles.reshape(CENTROIDS, D), energy)
```

```python
import math

import jax
import jax.numpy as jnp
from jax import lax
from jax.sharding import PartitionSpec as P

PASSES = 2
KAPPA = 64.0
ABSENT = 1.25
LIMIT = 1.125


def unit_vectors(values):
    wide = values.astype(jnp.float32)
    scale = lax.rsqrt(jnp.mean(wide * wide, axis=-1, keepdims=True) + 1e-06) * values.shape[-1] ** (
        -0.5
    )
    return (wide * scale).astype(jnp.bfloat16)


def contract_rows(left, right):
    return lax.dot_general(
        left, right, (((1,), (1,)), ((), ())), preferred_element_type=jnp.float32
    )


def contract_cols(left, right):
    return lax.dot_general(
        left, right, (((1,), (0,)), ((), ())), preferred_element_type=jnp.float32
    )


def partner_swap(value, mask, width):
    def branch(apart):
        if apart == 0:
            return lambda current: current
        return lambda current: lax.ppermute(current, "blk", [(i, i ^ apart) for i in range(width)])

    return lax.switch(mask, [branch(apart) for apart in range(width)], value)


def on_device(rows, block_ids, centroids, pairing):
    groups = lax.axis_size("dp")
    group_width = lax.axis_size("blk")
    devices = groups * group_width
    rows_dev, width = rows.shape
    tile_rows = centroids.shape[0]
    capacity = 2 * rows_dev // devices
    slot_count = devices * capacity
    owners = block_ids[:, 0]
    indicator = (owners[:, None] == jnp.arange(devices, dtype=jnp.int32)[None, :]).astype(jnp.int32)
    earlier = jnp.cumsum(indicator, axis=0, dtype=jnp.int32) - indicator
    place = jnp.sum(earlier * indicator, axis=1, dtype=jnp.int32)
    position = owners * capacity + place
    unit_rows = unit_vectors(rows)
    blank = jnp.where(jnp.arange(width)[None, :] == 0, ABSENT, 0.0).astype(jnp.bfloat16)
    outgoing = jnp.broadcast_to(blank, (slot_count, width)).at[position].set(unit_rows)
    chunks = outgoing.reshape(groups, group_width, capacity, width)

    def routed(mask):
        order = jnp.bitwise_xor(jnp.arange(group_width, dtype=jnp.int32), mask)
        sent = jnp.take(chunks, order, axis=1).reshape(devices, capacity, width)
        got = lax.all_to_all(sent, ("dp", "blk"), split_axis=0, concat_axis=0, tiled=True)
        return got.reshape(slot_count, width)

    own = lax.all_to_all(
        chunks.reshape(devices, capacity, width),
        ("dp", "blk"),
        split_axis=0,
        concat_axis=0,
        tiled=True,
    ).reshape(slot_count, width)
    others = [routed(pairing[p]) for p in range(PASSES)]
    own_here = own[:, 0] < LIMIT
    centers = centroids
    for p in range(PASSES):
        unit_tiles = unit_vectors(centers)
        other = others[p]
        other_here = other[:, 0] < LIMIT
        own_aff = jnp.exp(KAPPA * contract_rows(unit_tiles, own))
        other_aff = jnp.exp(KAPPA * contract_rows(unit_tiles, other))
        partial = jnp.stack([jnp.sum(own_aff, axis=0), jnp.sum(other_aff, axis=0)])
        swapped = partner_swap(partial, pairing[p], group_width)
        totals = partial[0] + swapped[1]
        other_totals = partial[1] + swapped[0]
        own_w = (own_aff * jnp.where(own_here, 1.0 / totals, 0.0)[None, :]).astype(jnp.bfloat16)
        other_w = (other_aff * jnp.where(other_here, 1.0 / other_totals, 0.0)[None, :]).astype(
            jnp.bfloat16
        )
        numerator = contract_cols(own_w, own) + contract_cols(other_w, other)
        counts = jnp.sum(own_w.astype(jnp.float32), axis=1) + jnp.sum(
            other_w.astype(jnp.float32), axis=1
        )
        centers = (
            math.sqrt(width)
            * (numerator + unit_tiles.astype(jnp.float32))
            / (counts + 1.0)[:, None]
        )
    slot_energy = jnp.log(totals / (2.0 * tile_rows))
    returned = lax.all_to_all(
        slot_energy.reshape(devices, capacity),
        ("dp", "blk"),
        split_axis=0,
        concat_axis=0,
        tiled=True,
    )
    energy = returned.reshape(slot_count)[position]
    return (centers, energy)


def solution(mesh):
    in_specs = (P(("dp", "blk"), None), P(("dp", "blk"), None), P(("dp", "blk"), None), P())
    out_specs = (P(("dp", "blk"), None), P(("dp", "blk")))
    return jax.shard_map(
        on_device, mesh=mesh, in_specs=in_specs, out_specs=out_specs, check_vma=False
    )
```

```python
import functools
import math

import jax
import jax.numpy as jnp
from jax import lax
from jax.experimental import pallas as pl
from jax.experimental.pallas import tpu as pltpu
from jax.sharding import PartitionSpec as P

PASSES = 2
KAPPA = 64.0
ABSENT = 1.25
LIMIT = 1.125
EPS = 1e-06
FLAG_ROWS = 16
VMEM = pltpu.VMEM
F32 = jnp.float32
BF16 = jnp.bfloat16


def unit_vectors(values):
    wide = values.astype(F32)
    scale = lax.rsqrt(jnp.mean(wide * wide, axis=-1, keepdims=True) + EPS) * values.shape[-1] ** (
        -0.5
    )
    return (wide * scale).astype(BF16)


def iota(shape, axis):
    return lax.broadcasted_iota(jnp.int32, shape, axis)


def dot(left, right, dims, precision=None):
    return lax.dot_general(
        left, right, (dims, ((), ())), preferred_element_type=F32, precision=precision
    )


def pack_kernel(
    capacity, pair_ref, ids_ref, rows_ref, out_ref, marks_ref, place_ref, unit_ref, spot_ref, y_ref
):
    g = pl.program_id(0)
    rows = rows_ref.shape[0]
    devices = marks_ref.shape[0]
    slots = y_ref.shape[0]
    members = slots // capacity

    @pl.when(g == 0)
    def _():
        unit_ref[...] = unit_vectors(rows_ref[...])
        hot = jnp.where(ids_ref[...] == iota((rows, devices), 1), 1.0, 0.0)
        marks = hot.T
        marks_ref[...] = marks.astype(BF16)
        before = jnp.where(iota((rows, rows), 0) < iota((rows, rows), 1), 1.0, 0.0).astype(BF16)
        seen = dot(marks.astype(BF16), before, ((1,), (0,)))
        place = jnp.sum(seen * marks, axis=0, keepdims=True)
        owner = jnp.sum(iota((devices, rows), 0).astype(F32) * marks, axis=0, keepdims=True)
        place_ref[...] = place.astype(jnp.int32)
        spot_ref[...] = (owner * capacity + place).astype(jnp.int32)

    chosen = jnp.where(iota((slots, rows), 0) + g * slots == spot_ref[...], 1.0, 0.0)
    found = jnp.sum(chosen, axis=1, keepdims=True)
    y = dot(chosen.astype(BF16), unit_ref[...], ((1,), (0,)))
    mark = jnp.where(iota((slots, 128), 1) == 0, ABSENT, 0.0) * (1.0 - found)
    y_ref[...] = y.astype(BF16)
    y_ref[:, :128] = (y[:, :128] + mark).astype(BF16)
    for k in range(members):
        out_ref[0, k, 0] = y_ref[k * capacity : (k + 1) * capacity, :]
        for p in range(PASSES):
            start = pl.multiple_of(jnp.bitwise_xor(pair_ref[p], k) * capacity, capacity)
            out_ref[0, k, 1 + p] = y_ref[pl.ds(start, capacity), :]


def pack(rows, block_ids, pairing, groups, members, capacity):
    count, width = rows.shape
    devices = groups * members
    return pl.pallas_call(
        functools.partial(pack_kernel, capacity),
        grid=(groups,),
        in_specs=[
            pl.BlockSpec(memory_space=pltpu.SMEM),
            pl.BlockSpec((count, 1), lambda g: (0, 0)),
            pl.BlockSpec((count, width), lambda g: (0, 0)),
        ],
        out_specs=[
            pl.BlockSpec(
                (1, members, 1 + PASSES, capacity, width), lambda g: (g, 0, 0, 0, 0)
            ),
            pl.BlockSpec((devices, count), lambda g: (0, 0)),
            pl.BlockSpec((1, count), lambda g: (0, 0)),
        ],
        out_shape=[
            jax.ShapeDtypeStruct((groups, members, 1 + PASSES, capacity, width), BF16),
            jax.ShapeDtypeStruct((devices, count), BF16),
            jax.ShapeDtypeStruct((1, count), jnp.int32),
        ],
        scratch_shapes=[
            VMEM((count, width), BF16),
            VMEM((1, count), jnp.int32),
            VMEM((members * capacity, width), BF16),
        ],
        cost_estimate=pl.CostEstimate(
            flops=4 * count * count * width, bytes_accessed=20 << 20, transcendentals=0
        ),
        name="pack",
    )(pairing, block_ids, rows)


def affinity_kernel(tiles_ref, x_ref, aff_ref, total_ref, flag_ref, wide_ref):
    tile_rows, width = tiles_ref.shape

    @pl.when((pl.program_id(0) == 0) & (pl.program_id(1) == 0))
    def _():
        wide_ref[:tile_rows] = tiles_ref[...]
        wide_ref[tile_rows:] = jnp.where(
            iota((FLAG_ROWS, width), 1) == 0, 1.0, 0.0
        ).astype(BF16)

    x = x_ref[...].reshape(-1, width)
    scores = dot(wide_ref[...], x, ((1,), (1,)))
    aff = jnp.exp(KAPPA * scores[:tile_rows])
    total_ref[0] = jnp.sum(aff, axis=0, keepdims=True)
    flag_ref[0] = scores[tile_rows : tile_rows + 1]
    aff_ref[0] = aff.astype(BF16)


def affinity(tiles, got, p, block):
    tile_rows, width = tiles.shape
    sources, _, capacity, _ = got.shape
    slots = sources * capacity
    steps = slots // block
    return pl.pallas_call(
        affinity_kernel,
        grid=(2, steps),
        in_specs=[
            pl.BlockSpec((tile_rows, width), lambda c, i: (0, 0)),
            pl.BlockSpec(
                (block // capacity, 1, capacity, width), lambda c, i: (i, c * (1 + p), 0, 0)
            ),
        ],
        out_specs=[
            pl.BlockSpec((1, tile_rows, block), lambda c, i: (c, 0, i)),
            pl.BlockSpec((1, 1, block), lambda c, i: (c, 0, i)),
            pl.BlockSpec((1, 1, block), lambda c, i: (c, 0, i)),
        ],
        out_shape=[
            jax.ShapeDtypeStruct((2, tile_rows, slots), BF16),
            jax.ShapeDtypeStruct((2, 1, slots), F32),
            jax.ShapeDtypeStruct((2, 1, slots), F32),
        ],
        scratch_shapes=[VMEM((tile_rows + FLAG_ROWS, width), BF16)],
        cost_estimate=pl.CostEstimate(
            flops=4 * slots * tile_rows * width,
            bytes_accessed=16 << 20,
            transcendentals=2 * slots * tile_rows,
        ),
        name="affinity",
    )(tiles, got)


def sums_kernel(
    last, tiles_ref, aff_ref, x_ref, total_ref, swapped_ref, flag_ref, out_ref, acc_ref, count_ref
):
    c, i = pl.program_id(0), pl.program_id(1)
    tile_rows, width = tiles_ref.shape
    block = aff_ref.shape[2]

    @pl.when((c == 0) & (i == 0))
    def _():
        acc_ref[...] = jnp.zeros_like(acc_ref)
        count_ref[...] = jnp.zeros_like(count_ref)

    total = total_ref[0] + swapped_ref[0]
    inverse = jnp.where(flag_ref[0] < LIMIT, 1.0 / total, 0.0)
    weights = aff_ref[0].astype(F32) * inverse
    part = weights[:, :128]
    for n in range(1, block // 128):
        part = part + weights[:, n * 128 : (n + 1) * 128]
    count_ref[...] += part
    acc_ref[...] += dot(weights.astype(BF16), x_ref[...].reshape(-1, width), ((1,), (0,)))

    @pl.when((c == pl.num_programs(0) - 1) & (i == pl.num_programs(1) - 1))
    def _():
        counts = jnp.sum(count_ref[...], axis=1, keepdims=True)
        centers = (
            math.sqrt(width) * (acc_ref[...] + tiles_ref[...].astype(F32)) / (counts + 1.0)
        )
        out_ref[...] = centers if last else unit_vectors(centers)


def sums(tiles, aff, got, total, swapped, flag, p, block):
    tile_rows, width = tiles.shape
    sources, _, capacity, _ = got.shape
    slots = sources * capacity
    last = p == PASSES - 1
    row_spec = pl.BlockSpec((1, 1, block), lambda c, i: (c, 0, i))
    return pl.pallas_call(
        functools.partial(sums_kernel, last),
        grid=(2, slots // block),
        in_specs=[
            pl.BlockSpec((tile_rows, width), lambda c, i: (0, 0)),
            pl.BlockSpec((1, tile_rows, block), lambda c, i: (c, 0, i)),
            pl.BlockSpec(
                (block // capacity, 1, capacity, width), lambda c, i: (i, c * (1 + p), 0, 0)
            ),
            row_spec,
            pl.BlockSpec((1, 1, block), lambda c, i: (1 - c, 0, i)),
            row_spec,
        ],
        out_specs=pl.BlockSpec((tile_rows, width), lambda c, i: (0, 0)),
        out_shape=jax.ShapeDtypeStruct((tile_rows, width), F32 if last else BF16),
        scratch_shapes=[VMEM((tile_rows, width), F32), VMEM((tile_rows, 128), F32)],
        cost_estimate=pl.CostEstimate(
            flops=4 * slots * tile_rows * width, bytes_accessed=16 << 20, transcendentals=0
        ),
        name="sums",
    )(tiles, aff, got, total, swapped, flag)


def spread_kernel(capacity, total_ref, swapped_ref, out_ref):
    sources, lanes = out_ref.shape
    slots = total_ref.shape[2]
    total = total_ref[0] + swapped_ref[1]
    picked = jnp.where(
        iota((sources, slots), 1) // capacity == iota((sources, slots), 0), total, 0.0
    )
    place = jnp.where(
        iota((slots, lanes), 0) % capacity == iota((slots, lanes), 1), 1.0, 0.0
    )
    out_ref[...] = dot(picked, place, ((1,), (0,)), lax.Precision.HIGHEST)


def spread(total, swapped, sources, capacity):
    return pl.pallas_call(
        functools.partial(spread_kernel, capacity),
        out_shape=jax.ShapeDtypeStruct((sources, 128), F32),
        name="spread",
    )(total, swapped)


def energy_kernel(capacity, columns, back_ref, marks_ref, place_ref, out_ref):
    back = back_ref[...].T[:capacity]
    found = dot(back, marks_ref[...].astype(F32), ((1,), (0,)), lax.Precision.HIGHEST)
    mine = jnp.where(iota(found.shape, 0) == place_ref[...], found, 0.0)
    total = jnp.sum(mine, axis=0, keepdims=True)
    out_ref[...] = jnp.log(total / columns)


def energies(back, marks, place, capacity, columns):
    return pl.pallas_call(
        functools.partial(energy_kernel, capacity, columns),
        out_shape=jax.ShapeDtypeStruct(place.shape, F32),
        name="energies",
    )(back, marks, place)


def partner_swap(value, mask, width):
    def branch(apart):
        if apart == 0:
            return lambda current: current
        return lambda current: lax.ppermute(current, "blk", [(i, i ^ apart) for i in range(width)])

    return lax.switch(mask, [branch(apart) for apart in range(width)], value)


def on_device(rows, block_ids, centroids, pairing):
    groups = lax.axis_size("dp")
    members = lax.axis_size("blk")
    devices = groups * members
    rows_dev, width = rows.shape
    tile_rows = centroids.shape[0]
    capacity = 2 * rows_dev // devices
    sent, marks, place = pack(rows, block_ids, pairing, groups, members, capacity)
    got = lax.all_to_all(
        sent.reshape(devices, (1 + PASSES) * capacity, width),
        ("dp", "blk"),
        split_axis=0,
        concat_axis=0,
        tiled=True,
    ).reshape(devices, 1 + PASSES, capacity, width)
    tiles = unit_vectors(centroids)
    for p in range(PASSES):
        aff, total, flag = affinity(tiles, got, p, 512)
        swapped = partner_swap(total, pairing[p], members)
        if p == PASSES - 1:
            back = lax.all_to_all(
                spread(total, swapped, devices, capacity),
                ("dp", "blk"),
                split_axis=0,
                concat_axis=0,
                tiled=True,
            )
        tiles = sums(tiles, aff, got, total, swapped, flag, p, 512)
    energy = energies(back, marks, place, capacity, 2.0 * tile_rows)
    return (tiles, energy.reshape(rows_dev))


def solution(mesh):
    in_specs = (P(("dp", "blk"), None), P(("dp", "blk"), None), P(("dp", "blk"), None), P())
    out_specs = (P(("dp", "blk"), None), P(("dp", "blk")))
    return jax.shard_map(
        on_device, mesh=mesh, in_specs=in_specs, out_specs=out_specs, check_vma=False
    )
```

```python
import functools
import math

import jax
import jax.numpy as jnp
from jax import lax
from jax.experimental import pallas as pl
from jax.experimental.pallas import tpu as pltpu
from jax.sharding import PartitionSpec as P

PASSES = 2
KAPPA = 64.0
ABSENT = 1.25
LIMIT = 1.125
EPS = 1e-06
FLAG_ROWS = 16
VMEM = pltpu.VMEM
F32 = jnp.float32
BF16 = jnp.bfloat16


def unit_vectors(values):
    wide = values.astype(F32)
    scale = lax.rsqrt(jnp.mean(wide * wide, axis=-1, keepdims=True) + EPS) * values.shape[-1] ** (
        -0.5
    )
    return (wide * scale).astype(BF16)


def iota(shape, axis):
    return lax.broadcasted_iota(jnp.int32, shape, axis)


def dot(left, right, dims, precision=None):
    return lax.dot_general(
        left, right, (dims, ((), ())), preferred_element_type=F32, precision=precision
    )


def pack_kernel(
    capacity, pair_ref, ids_ref, rows_ref, out_ref, marks_ref, place_ref, unit_ref, spot_ref, y_ref
):
    g = pl.program_id(0)
    rows = rows_ref.shape[0]
    devices = marks_ref.shape[0]
    slots = y_ref.shape[0]
    groups, members = out_ref.shape[:2]

    @pl.when(g == 0)
    def _():
        unit_ref[...] = unit_vectors(rows_ref[...])
        marks = jnp.where(ids_ref[...] == iota((devices, rows), 0), 1.0, 0.0)
        marks_ref[...] = marks.astype(BF16)
        pieces = [marks[:, n : n + 128] for n in range(0, rows, 128)]
        before = jnp.where(iota((128, 128), 0) < iota((128, 128), 1), 1.0, 0.0).astype(BF16)
        seen = dot(jnp.concatenate(pieces, axis=0).astype(BF16), before, ((1,), (0,)))
        whose = iota((devices, 128), 0).astype(F32)
        passed = jnp.zeros((devices, 1), F32)
        for n, piece in enumerate(pieces):
            lanes = slice(n * 128, (n + 1) * 128)
            here = seen[n * devices : (n + 1) * devices] + passed
            place = jnp.sum(here * piece, axis=0, keepdims=True)
            owner = jnp.sum(whose * piece, axis=0, keepdims=True)
            place_ref[:, lanes] = place.astype(jnp.int32)
            spot_ref[:, lanes] = (owner * capacity + place).astype(jnp.int32)
            passed = passed + jnp.sum(piece, axis=1, keepdims=True)

    chosen = jnp.where(iota((slots, rows), 0) + g * slots == spot_ref[...], 1.0, 0.0)
    found = jnp.sum(chosen, axis=1, keepdims=True)
    y = dot(chosen.astype(BF16), unit_ref[...], ((1,), (0,)))
    mark = jnp.where(iota((slots, 128), 1) == 0, ABSENT, 0.0) * (1.0 - found)
    y_ref[...] = y.astype(BF16)
    y_ref[:, :128] = (y[:, :128] + mark).astype(BF16)
    for h in range(groups):
        base = h * members * capacity
        for k in range(members):
            out_ref[h, k, 0] = y_ref[base + k * capacity : base + (k + 1) * capacity, :]
            for p in range(PASSES):
                start = base + jnp.bitwise_xor(pair_ref[p], k) * capacity
                out_ref[h, k, 1 + p] = y_ref[pl.ds(pl.multiple_of(start, capacity), capacity), :]


def pack(rows, block_ids, pairing, groups, members, capacity, steps):
    count, width = rows.shape
    devices = groups * members
    return pl.pallas_call(
        functools.partial(pack_kernel, capacity),
        grid=(steps,),
        in_specs=[
            pl.BlockSpec(memory_space=pltpu.SMEM),
            pl.BlockSpec((1, count), lambda g: (0, 0)),
            pl.BlockSpec((count, width), lambda g: (0, 0)),
        ],
        out_specs=[
            pl.BlockSpec(
                (groups // steps, members, 1 + PASSES, capacity, width),
                lambda g: (g, 0, 0, 0, 0),
            ),
            pl.BlockSpec((devices, count), lambda g: (0, 0)),
            pl.BlockSpec((1, count), lambda g: (0, 0)),
        ],
        out_shape=[
            jax.ShapeDtypeStruct((groups, members, 1 + PASSES, capacity, width), BF16),
            jax.ShapeDtypeStruct((devices, count), BF16),
            jax.ShapeDtypeStruct((1, count), jnp.int32),
        ],
        scratch_shapes=[
            VMEM((count, width), BF16),
            VMEM((1, count), jnp.int32),
            VMEM((devices * capacity // steps, width), BF16),
        ],
        cost_estimate=pl.CostEstimate(
            flops=4 * count * count * width, bytes_accessed=20 << 20, transcendentals=0
        ),
        name="pack",
    )(pairing, block_ids.reshape(1, count), rows)


def affinity_kernel(last, inner, tiles_ref, x_ref, aff_ref, total_ref, flag_ref, *rest):
    wide_ref = rest[-1]
    tile_rows, width = tiles_ref.shape
    capacity = x_ref.shape[2]
    block = aff_ref.shape[2]

    @pl.when((pl.program_id(0) == 0) & (pl.program_id(1) == 0))
    def _():
        wide_ref[:tile_rows] = tiles_ref[...]
        wide_ref[tile_rows:] = jnp.where(
            iota((FLAG_ROWS, width), 1) == 0, 1.0, 0.0
        ).astype(BF16)

    count = inner // capacity
    for n in range(block // inner):
        lanes = slice(n * inner, (n + 1) * inner)
        x = x_ref[n * count : (n + 1) * count].reshape(inner, width)
        scores = dot(wide_ref[...], x, ((1,), (1,)))
        aff = jnp.exp2((KAPPA * math.log2(math.e)) * scores[:tile_rows])
        total = jnp.sum(aff, axis=0, keepdims=True)
        total_ref[0, :, lanes] = total
        flag_ref[0, :, lanes] = scores[tile_rows : tile_rows + 1]
        aff_ref[0, :, lanes] = aff.astype(BF16)
        if last:
            for v in range(inner // 128):
                piece = total[:, v * 128 : (v + 1) * 128]
                for k in range(128 // capacity):
                    source = (n * inner + v * 128) // capacity + k
                    rest[0][source] = pltpu.roll(piece, (128 - k * capacity) % 128, 1)


def affinity(tiles, got, p, block, inner):
    tile_rows, width = tiles.shape
    sources, _, capacity, _ = got.shape
    slots = sources * capacity
    last = p == PASSES - 1
    row_spec = pl.BlockSpec((1, 1, block), lambda c, i: (c, 0, i))
    row_shape = jax.ShapeDtypeStruct((2, 1, slots), F32)
    out_specs = [pl.BlockSpec((1, tile_rows, block), lambda c, i: (c, 0, i)), row_spec, row_spec]
    out_shape = [jax.ShapeDtypeStruct((2, tile_rows, slots), BF16), row_shape, row_shape]
    if last:
        out_specs.append(pl.BlockSpec((block // capacity, 1, 128), lambda c, i: (i, 0, c)))
        out_shape.append(jax.ShapeDtypeStruct((sources, 1, 256), F32))
    return pl.pallas_call(
        functools.partial(affinity_kernel, last, inner),
        grid=(2, slots // block),
        in_specs=[
            pl.BlockSpec((tile_rows, width), lambda c, i: (0, 0)),
            pl.BlockSpec(
                (block // capacity, 1, capacity, width), lambda c, i: (i, c * (1 + p), 0, 0)
            ),
        ],
        out_specs=out_specs,
        out_shape=out_shape,
        scratch_shapes=[VMEM((tile_rows + FLAG_ROWS, width), BF16)],
        cost_estimate=pl.CostEstimate(
            flops=4 * slots * tile_rows * width,
            bytes_accessed=16 << 20,
            transcendentals=2 * slots * tile_rows,
        ),
        name="affinity",
    )(tiles, got)


def sums_kernel(
    last, tiles_ref, aff_ref, x_ref, total_ref, swapped_ref, flag_ref, out_ref, acc_ref, count_ref
):
    c, i = pl.program_id(0), pl.program_id(1)
    tile_rows, width = tiles_ref.shape
    block = aff_ref.shape[2]

    @pl.when((c == 0) & (i == 0))
    def _():
        acc_ref[...] = jnp.zeros_like(acc_ref)
        count_ref[...] = jnp.zeros_like(count_ref)

    total = total_ref[0] + swapped_ref[0]
    inverse = jnp.where(flag_ref[0] < LIMIT, 1.0 / total, 0.0)
    weights = aff_ref[0].astype(F32) * inverse
    part = weights[:, :128]
    for n in range(1, block // 128):
        part = part + weights[:, n * 128 : (n + 1) * 128]
    count_ref[...] += part
    acc_ref[...] += dot(weights.astype(BF16), x_ref[...].reshape(-1, width), ((1,), (0,)))

    @pl.when((c == pl.num_programs(0) - 1) & (i == pl.num_programs(1) - 1))
    def _():
        counts = jnp.sum(count_ref[...], axis=1, keepdims=True)
        centers = (
            math.sqrt(width) * (acc_ref[...] + tiles_ref[...].astype(F32)) / (counts + 1.0)
        )
        out_ref[...] = centers if last else unit_vectors(centers)


def sums(tiles, aff, got, total, swapped, flag, p, block):
    tile_rows, width = tiles.shape
    sources, _, capacity, _ = got.shape
    slots = sources * capacity
    last = p == PASSES - 1
    row_spec = pl.BlockSpec((1, 1, block), lambda c, i: (c, 0, i))
    return pl.pallas_call(
        functools.partial(sums_kernel, last),
        grid=(2, slots // block),
        in_specs=[
            pl.BlockSpec((tile_rows, width), lambda c, i: (0, 0)),
            pl.BlockSpec((1, tile_rows, block), lambda c, i: (c, 0, i)),
            pl.BlockSpec(
                (block // capacity, 1, capacity, width), lambda c, i: (i, c * (1 + p), 0, 0)
            ),
            row_spec,
            pl.BlockSpec((1, 1, block), lambda c, i: (1 - c, 0, i)),
            row_spec,
        ],
        out_specs=pl.BlockSpec((tile_rows, width), lambda c, i: (0, 0)),
        out_shape=jax.ShapeDtypeStruct((tile_rows, width), F32 if last else BF16),
        scratch_shapes=[VMEM((tile_rows, width), F32), VMEM((tile_rows, 128), F32)],
        cost_estimate=pl.CostEstimate(
            flops=4 * slots * tile_rows * width, bytes_accessed=16 << 20, transcendentals=0
        ),
        name="sums",
    )(tiles, aff, got, total, swapped, flag)


def energy_kernel(capacity, columns, pair_ref, back_ref, marks_ref, place_ref, out_ref):
    devices = back_ref.shape[0]
    across = jnp.where(
        jnp.bitwise_xor(iota((devices, devices), 0), pair_ref[PASSES - 1])
        == iota((devices, devices), 1),
        1.0,
        0.0,
    )
    total = back_ref[:, 0, :128] + dot(
        across, back_ref[:, 0, 128:], ((1,), (0,)), lax.Precision.HIGHEST
    )
    found = dot(
        total.T[:capacity], marks_ref[...].astype(F32), ((1,), (0,)), lax.Precision.HIGHEST
    )
    mine = jnp.where(iota(found.shape, 0) == place_ref[...], found, 0.0)
    out_ref[...] = jnp.log(jnp.sum(mine, axis=0, keepdims=True) / columns)


def energies(pairing, back, marks, place, capacity, columns):
    whole = pl.BlockSpec(memory_space=VMEM)
    return pl.pallas_call(
        functools.partial(energy_kernel, capacity, columns),
        in_specs=[pl.BlockSpec(memory_space=pltpu.SMEM), whole, whole, whole],
        out_specs=whole,
        out_shape=jax.ShapeDtypeStruct(place.shape, F32),
        name="energies",
    )(pairing, back, marks, place)


def partner_swap(value, mask, width):
    def branch(apart):
        if apart == 0:
            return lambda current: current
        return lambda current: lax.ppermute(current, "blk", [(i, i ^ apart) for i in range(width)])

    return lax.switch(mask, [branch(apart) for apart in range(width)], value)


def on_device(rows, block_ids, centroids, pairing):
    groups = lax.axis_size("dp")
    members = lax.axis_size("blk")
    devices = groups * members
    rows_dev, width = rows.shape
    tile_rows = centroids.shape[0]
    capacity = 2 * rows_dev // devices
    sent, marks, place = pack(rows, block_ids, pairing, groups, members, capacity, 2)
    got = lax.all_to_all(
        sent.reshape(devices, (1 + PASSES) * capacity, width),
        ("dp", "blk"),
        split_axis=0,
        concat_axis=0,
        tiled=True,
    ).reshape(devices, 1 + PASSES, capacity, width)
    tiles = unit_vectors(centroids)
    for p in range(PASSES):
        aff, total, flag, *spread = affinity(tiles, got, p, 1024, 512)
        if spread:
            back = lax.all_to_all(
                spread[0], ("dp", "blk"), split_axis=0, concat_axis=0, tiled=True
            )
        swapped = partner_swap(total, pairing[p], members)
        tiles = sums(tiles, aff, got, total, swapped, flag, p, 1024)
    energy = energies(pairing, back, marks, place, capacity, 2.0 * tile_rows)
    return (tiles, energy.reshape(rows_dev))


def solution(mesh):
    in_specs = (P(("dp", "blk"), None), P(("dp", "blk"), None), P(("dp", "blk"), None), P())
    out_specs = (P(("dp", "blk"), None), P(("dp", "blk")))
    return jax.shard_map(
        on_device, mesh=mesh, in_specs=in_specs, out_specs=out_specs, check_vma=False
    )
```

```python
import functools
import math

import jax
import jax.numpy as jnp
from jax import lax
from jax.experimental import pallas as pl
from jax.experimental.pallas import tpu as pltpu
from jax.sharding import PartitionSpec as P

PASSES = 2
KAPPA = 64.0
ABSENT = 1.25
LIMIT = 1.125
EPS = 1e-06
FLAG_ROWS = 16
VMEM = pltpu.VMEM
F32 = jnp.float32
BF16 = jnp.bfloat16


def unit_vectors(values):
    wide = values.astype(F32)
    scale = lax.rsqrt(jnp.mean(wide * wide, axis=-1, keepdims=True) + EPS) * values.shape[-1] ** (
        -0.5
    )
    return (wide * scale).astype(BF16)


def iota(shape, axis):
    return lax.broadcasted_iota(jnp.int32, shape, axis)


def dot(left, right, dims, precision=None):
    return lax.dot_general(
        left, right, (dims, ((), ())), preferred_element_type=F32, precision=precision
    )


def pack_kernel(
    capacity,
    pair_ref,
    ids_ref,
    rows_ref,
    tiles_ref,
    out_ref,
    marks_ref,
    place_ref,
    units_ref,
    unit_ref,
    spot_ref,
    y_ref,
):
    g = pl.program_id(0)
    rows = rows_ref.shape[0]
    devices = marks_ref.shape[0]
    slots = y_ref.shape[0]
    groups, members = out_ref.shape[:2]

    @pl.when(g == 0)
    def _():
        unit_ref[...] = unit_vectors(rows_ref[...])
        marks = jnp.where(ids_ref[...] == iota((devices, rows), 0), 1.0, 0.0)
        marks_ref[...] = marks.astype(BF16)
        pieces = [marks[:, n : n + 128] for n in range(0, rows, 128)]
        before = jnp.where(iota((128, 128), 0) < iota((128, 128), 1), 1.0, 0.0).astype(BF16)
        seen = dot(jnp.concatenate(pieces, axis=0).astype(BF16), before, ((1,), (0,)))
        whose = iota((devices, 128), 0).astype(F32)
        passed = jnp.zeros((devices, 1), F32)
        for n, piece in enumerate(pieces):
            lanes = slice(n * 128, (n + 1) * 128)
            here = seen[n * devices : (n + 1) * devices] + passed
            place = jnp.sum(here * piece, axis=0, keepdims=True)
            owner = jnp.sum(whose * piece, axis=0, keepdims=True)
            place_ref[:, lanes] = place.astype(jnp.int32)
            spot_ref[:, lanes] = (owner * capacity + place).astype(jnp.int32)
            passed = passed + jnp.sum(piece, axis=1, keepdims=True)

    units_ref[...] = unit_vectors(tiles_ref[...])
    chosen = jnp.where(iota((slots, rows), 0) + g * slots == spot_ref[...], 1.0, 0.0)
    found = jnp.sum(chosen, axis=1, keepdims=True)
    y = dot(chosen.astype(BF16), unit_ref[...], ((1,), (0,)))
    mark = jnp.where(iota((slots, 128), 1) == 0, ABSENT, 0.0) * (1.0 - found)
    y_ref[...] = y.astype(BF16)
    y_ref[:, :128] = (y[:, :128] + mark).astype(BF16)
    for h in range(groups):
        base = h * members * capacity
        for k in range(members):
            out_ref[h, k, 0] = y_ref[base + k * capacity : base + (k + 1) * capacity, :]
            for p in range(PASSES):
                start = base + jnp.bitwise_xor(pair_ref[p], k) * capacity
                out_ref[h, k, 1 + p] = y_ref[pl.ds(pl.multiple_of(start, capacity), capacity), :]


def pack(rows, block_ids, centroids, pairing, groups, members, capacity, steps):
    count, width = rows.shape
    tile_spec = pl.BlockSpec((centroids.shape[0] // steps, width), lambda g: (g, 0))
    devices = groups * members
    return pl.pallas_call(
        functools.partial(pack_kernel, capacity),
        grid=(steps,),
        in_specs=[
            pl.BlockSpec(memory_space=pltpu.SMEM),
            pl.BlockSpec((1, count), lambda g: (0, 0)),
            pl.BlockSpec((count, width), lambda g: (0, 0)),
            tile_spec,
        ],
        out_specs=[
            pl.BlockSpec(
                (groups // steps, members, 1 + PASSES, capacity, width),
                lambda g: (g, 0, 0, 0, 0),
            ),
            pl.BlockSpec((devices, count), lambda g: (0, 0)),
            pl.BlockSpec((1, count), lambda g: (0, 0)),
            tile_spec,
        ],
        out_shape=[
            jax.ShapeDtypeStruct((groups, members, 1 + PASSES, capacity, width), BF16),
            jax.ShapeDtypeStruct((devices, count), BF16),
            jax.ShapeDtypeStruct((1, count), jnp.int32),
            jax.ShapeDtypeStruct(centroids.shape, BF16),
        ],
        scratch_shapes=[
            VMEM((count, width), BF16),
            VMEM((1, count), jnp.int32),
            VMEM((devices * capacity // steps, width), BF16),
        ],
        cost_estimate=pl.CostEstimate(
            flops=4 * count * count * width, bytes_accessed=20 << 20, transcendentals=0
        ),
        name="pack",
    )(pairing, block_ids.reshape(1, count), rows, centroids)


def affinity_kernel(last, inner, tiles_ref, x_ref, aff_ref, total_ref, flag_ref, *rest):
    wide_ref = rest[-1]
    tile_rows, width = tiles_ref.shape
    capacity = x_ref.shape[2]
    block = aff_ref.shape[2]

    @pl.when((pl.program_id(0) == 0) & (pl.program_id(1) == 0))
    def _():
        wide_ref[:tile_rows] = tiles_ref[...]
        wide_ref[tile_rows:] = jnp.where(
            iota((FLAG_ROWS, width), 1) == 0, 1.0, 0.0
        ).astype(BF16)

    count = inner // capacity
    for n in range(block // inner):
        lanes = slice(n * inner, (n + 1) * inner)
        x = x_ref[n * count : (n + 1) * count].reshape(inner, width)
        scores = dot(wide_ref[...], x, ((1,), (1,)))
        aff = jnp.exp2((KAPPA * math.log2(math.e)) * scores[:tile_rows])
        total = jnp.sum(aff, axis=0, keepdims=True)
        total_ref[0, :, lanes] = total
        flag_ref[0, :, lanes] = scores[tile_rows : tile_rows + 1]
        aff_ref[0, :, lanes] = aff.astype(BF16)
        if last:
            for v in range(inner // 128):
                piece = total[:, v * 128 : (v + 1) * 128]
                for k in range(128 // capacity):
                    source = (n * inner + v * 128) // capacity + k
                    rest[0][source] = pltpu.roll(piece, (128 - k * capacity) % 128, 1)


def affinity(tiles, got, p, block, inner):
    tile_rows, width = tiles.shape
    sources, _, capacity, _ = got.shape
    slots = sources * capacity
    last = p == PASSES - 1
    row_spec = pl.BlockSpec((1, 1, block), lambda c, i: (c, 0, i))
    row_shape = jax.ShapeDtypeStruct((2, 1, slots), F32)
    out_specs = [pl.BlockSpec((1, tile_rows, block), lambda c, i: (c, 0, i)), row_spec, row_spec]
    out_shape = [jax.ShapeDtypeStruct((2, tile_rows, slots), BF16), row_shape, row_shape]
    if last:
        out_specs.append(pl.BlockSpec((block // capacity, 1, 128), lambda c, i: (i, 0, c)))
        out_shape.append(jax.ShapeDtypeStruct((sources, 1, 256), F32))
    return pl.pallas_call(
        functools.partial(affinity_kernel, last, inner),
        grid=(2, slots // block),
        in_specs=[
            pl.BlockSpec((tile_rows, width), lambda c, i: (0, 0)),
            pl.BlockSpec(
                (block // capacity, 1, capacity, width), lambda c, i: (i, c * (1 + p), 0, 0)
            ),
        ],
        out_specs=out_specs,
        out_shape=out_shape,
        scratch_shapes=[VMEM((tile_rows + FLAG_ROWS, width), BF16)],
        cost_estimate=pl.CostEstimate(
            flops=4 * slots * tile_rows * width,
            bytes_accessed=16 << 20,
            transcendentals=2 * slots * tile_rows,
        ),
        name="affinity",
    )(tiles, got)


def sums_kernel(
    last, tiles_ref, aff_ref, x_ref, total_ref, swapped_ref, flag_ref, out_ref, acc_ref, count_ref
):
    c, i = pl.program_id(0), pl.program_id(1)
    tile_rows, width = tiles_ref.shape
    block = aff_ref.shape[2]

    @pl.when((c == 0) & (i == 0))
    def _():
        acc_ref[...] = jnp.zeros_like(acc_ref)
        count_ref[...] = jnp.zeros_like(count_ref)

    total = total_ref[0] + swapped_ref[0]
    inverse = jnp.where(flag_ref[0] < LIMIT, 1.0 / total, 0.0)
    weights = aff_ref[0].astype(F32) * inverse
    part = weights[:, :128]
    for n in range(1, block // 128):
        part = part + weights[:, n * 128 : (n + 1) * 128]
    count_ref[...] += part
    acc_ref[...] += dot(weights.astype(BF16), x_ref[...].reshape(-1, width), ((1,), (0,)))

    @pl.when((c == pl.num_programs(0) - 1) & (i == pl.num_programs(1) - 1))
    def _():
        counts = jnp.sum(count_ref[...], axis=1, keepdims=True)
        centers = (
            math.sqrt(width) * (acc_ref[...] + tiles_ref[...].astype(F32)) / (counts + 1.0)
        )
        out_ref[...] = centers if last else unit_vectors(centers)


def sums(tiles, aff, got, total, swapped, flag, p, block):
    tile_rows, width = tiles.shape
    sources, _, capacity, _ = got.shape
    slots = sources * capacity
    last = p == PASSES - 1
    row_spec = pl.BlockSpec((1, 1, block), lambda c, i: (c, 0, i))
    return pl.pallas_call(
        functools.partial(sums_kernel, last),
        grid=(2, slots // block),
        in_specs=[
            pl.BlockSpec((tile_rows, width), lambda c, i: (0, 0)),
            pl.BlockSpec((1, tile_rows, block), lambda c, i: (c, 0, i)),
            pl.BlockSpec(
                (block // capacity, 1, capacity, width), lambda c, i: (i, c * (1 + p), 0, 0)
            ),
            row_spec,
            pl.BlockSpec((1, 1, block), lambda c, i: (1 - c, 0, i)),
            row_spec,
        ],
        out_specs=pl.BlockSpec((tile_rows, width), lambda c, i: (0, 0)),
        out_shape=jax.ShapeDtypeStruct((tile_rows, width), F32 if last else BF16),
        scratch_shapes=[VMEM((tile_rows, width), F32), VMEM((tile_rows, 128), F32)],
        cost_estimate=pl.CostEstimate(
            flops=4 * slots * tile_rows * width, bytes_accessed=16 << 20, transcendentals=0
        ),
        name="sums",
    )(tiles, aff, got, total, swapped, flag)


def thirds(values):
    high = values.astype(BF16)
    rest = values - high.astype(F32)
    middle = rest.astype(BF16)
    low = (rest - middle.astype(F32)).astype(BF16)
    return jnp.concatenate([high, middle, low], axis=0)


def energy_kernel(capacity, columns, pair_ref, back_ref, marks_ref, place_ref, out_ref):
    devices = back_ref.shape[0]
    across = jnp.where(
        jnp.bitwise_xor(iota((devices, devices), 0), pair_ref[PASSES - 1])
        == iota((devices, devices), 1),
        1.0,
        0.0,
    )
    own = thirds(back_ref[:, 0, :128].T[:capacity])
    other = thirds(back_ref[:, 0, 128:].T[:capacity])
    other = dot(other, across.astype(BF16), ((1,), (0,))).astype(BF16)
    found = dot(jnp.concatenate([own, other], axis=0), marks_ref[...], ((1,), (0,)))
    sums = found[:capacity]
    for n in range(1, 6):
        sums = sums + found[n * capacity : (n + 1) * capacity]
    mine = jnp.where(iota(sums.shape, 0) == place_ref[...], sums, 0.0)
    out_ref[...] = jnp.log(jnp.sum(mine, axis=0, keepdims=True) / columns)


def energies(pairing, back, marks, place, capacity, columns):
    whole = pl.BlockSpec(memory_space=VMEM)
    return pl.pallas_call(
        functools.partial(energy_kernel, capacity, columns),
        in_specs=[pl.BlockSpec(memory_space=pltpu.SMEM), whole, whole, whole],
        out_specs=whole,
        out_shape=jax.ShapeDtypeStruct(place.shape, F32),
        name="energies",
    )(pairing, back, marks, place)


def partner_swap(value, mask, width):
    def branch(apart):
        if apart == 0:
            return lambda current: current
        return lambda current: lax.ppermute(current, "blk", [(i, i ^ apart) for i in range(width)])

    return lax.switch(mask, [branch(apart) for apart in range(width)], value)


def on_device(rows, block_ids, centroids, pairing):
    groups = lax.axis_size("dp")
    members = lax.axis_size("blk")
    devices = groups * members
    rows_dev, width = rows.shape
    tile_rows = centroids.shape[0]
    capacity = 2 * rows_dev // devices
    sent, marks, place, tiles = pack(
        rows, block_ids, centroids, pairing, groups, members, capacity, 4
    )
    got = lax.all_to_all(
        sent.reshape(devices, (1 + PASSES) * capacity, width),
        ("dp", "blk"),
        split_axis=0,
        concat_axis=0,
        tiled=True,
    ).reshape(devices, 1 + PASSES, capacity, width)
    got, pairing = lax.optimization_barrier((got, pairing))
    for p in range(PASSES):
        aff, total, flag, *spread = affinity(tiles, got, p, 1024, 512)
        if spread:
            back = lax.all_to_all(
                spread[0], ("dp", "blk"), split_axis=0, concat_axis=0, tiled=True
            )
        swapped = partner_swap(total, pairing[p], members)
        tiles = sums(tiles, aff, got, total, swapped, flag, p, 1024)
    energy = energies(pairing, back, marks, place, capacity, 2.0 * tile_rows)
    return (tiles, energy.reshape(rows_dev))


def solution(mesh):
    in_specs = (P(("dp", "blk"), None), P(("dp", "blk"), None), P(("dp", "blk"), None), P())
    out_specs = (P(("dp", "blk"), None), P(("dp", "blk")))
    return jax.shard_map(
        on_device, mesh=mesh, in_specs=in_specs, out_specs=out_specs, check_vma=False
    )
```

```python
import functools
import math

import jax
import jax.numpy as jnp
from jax import lax
from jax.experimental import pallas as pl
from jax.experimental.pallas import tpu as pltpu
from jax.sharding import PartitionSpec as P

PASSES = 2
KAPPA = 64.0
ABSENT = 1.25
LIMIT = 1.125
EPS = 1e-06
FLAG_ROWS = 16
VMEM = pltpu.VMEM
F32 = jnp.float32
BF16 = jnp.bfloat16


def unit_vectors(values):
    wide = values.astype(F32)
    scale = lax.rsqrt(jnp.mean(wide * wide, axis=-1, keepdims=True) + EPS) * values.shape[-1] ** (
        -0.5
    )
    return (wide * scale).astype(BF16)


def iota(shape, axis):
    return lax.broadcasted_iota(jnp.int32, shape, axis)


def dot(left, right, dims, precision=None):
    return lax.dot_general(
        left, right, (dims, ((), ())), preferred_element_type=F32, precision=precision
    )


def pack_kernel(
    capacity,
    pair_ref,
    ids_ref,
    rows_ref,
    tiles_ref,
    out_ref,
    late_ref,
    marks_ref,
    place_ref,
    units_ref,
    unit_ref,
    spot_ref,
    y_ref,
):
    g = pl.program_id(0)
    rows = rows_ref.shape[0]
    devices = marks_ref.shape[0]
    slots = y_ref.shape[0]
    groups, members = out_ref.shape[:2]

    @pl.when(g == 0)
    def _():
        unit_ref[...] = unit_vectors(rows_ref[...])
        marks = jnp.where(ids_ref[...] == iota((devices, rows), 0), 1.0, 0.0)
        marks_ref[...] = marks.astype(BF16)
        pieces = [marks[:, n : n + 128] for n in range(0, rows, 128)]
        before = jnp.where(iota((128, 128), 0) < iota((128, 128), 1), 1.0, 0.0).astype(BF16)
        seen = dot(jnp.concatenate(pieces, axis=0).astype(BF16), before, ((1,), (0,)))
        whose = iota((devices, 128), 0).astype(F32)
        passed = jnp.zeros((devices, 1), F32)
        for n, piece in enumerate(pieces):
            lanes = slice(n * 128, (n + 1) * 128)
            here = seen[n * devices : (n + 1) * devices] + passed
            place = jnp.sum(here * piece, axis=0, keepdims=True)
            owner = jnp.sum(whose * piece, axis=0, keepdims=True)
            place_ref[:, lanes] = place.astype(jnp.int32)
            spot_ref[:, lanes] = (owner * capacity + place).astype(jnp.int32)
            passed = passed + jnp.sum(piece, axis=1, keepdims=True)

    units_ref[...] = unit_vectors(tiles_ref[...])
    chosen = jnp.where(iota((slots, rows), 0) + g * slots == spot_ref[...], 1.0, 0.0)
    found = jnp.sum(chosen, axis=1, keepdims=True)
    y = dot(chosen.astype(BF16), unit_ref[...], ((1,), (0,)))
    mark = jnp.where(iota((slots, 128), 1) == 0, ABSENT, 0.0) * (1.0 - found)
    y_ref[...] = y.astype(BF16)
    y_ref[:, :128] = (y[:, :128] + mark).astype(BF16)
    for h in range(groups):
        base = h * members * capacity
        for k in range(members):
            out_ref[h, k, 0] = y_ref[base + k * capacity : base + (k + 1) * capacity, :]
            for p in range(PASSES):
                start = base + jnp.bitwise_xor(pair_ref[p], k) * capacity
                chunk = y_ref[pl.ds(pl.multiple_of(start, capacity), capacity), :]
                if p == 0:
                    out_ref[h, k, 1] = chunk
                else:
                    late_ref[h, k] = chunk


def pack(rows, block_ids, centroids, pairing, groups, members, capacity, steps):
    count, width = rows.shape
    tile_spec = pl.BlockSpec((centroids.shape[0] // steps, width), lambda g: (g, 0))
    devices = groups * members
    return pl.pallas_call(
        functools.partial(pack_kernel, capacity),
        grid=(steps,),
        in_specs=[
            pl.BlockSpec(memory_space=pltpu.SMEM),
            pl.BlockSpec((1, count), lambda g: (0, 0)),
            pl.BlockSpec((count, width), lambda g: (0, 0)),
            tile_spec,
        ],
        out_specs=[
            pl.BlockSpec(
                (groups // steps, members, 2, capacity, width), lambda g: (g, 0, 0, 0, 0)
            ),
            pl.BlockSpec((groups // steps, members, capacity, width), lambda g: (g, 0, 0, 0)),
            pl.BlockSpec((devices, count), lambda g: (0, 0)),
            pl.BlockSpec((1, count), lambda g: (0, 0)),
            tile_spec,
        ],
        out_shape=[
            jax.ShapeDtypeStruct((groups, members, 2, capacity, width), BF16),
            jax.ShapeDtypeStruct((groups, members, capacity, width), BF16),
            jax.ShapeDtypeStruct((devices, count), BF16),
            jax.ShapeDtypeStruct((1, count), jnp.int32),
            jax.ShapeDtypeStruct(centroids.shape, BF16),
        ],
        scratch_shapes=[
            VMEM((count, width), BF16),
            VMEM((1, count), jnp.int32),
            VMEM((devices * capacity // steps, width), BF16),
        ],
        cost_estimate=pl.CostEstimate(
            flops=4 * count * count * width, bytes_accessed=20 << 20, transcendentals=0
        ),
        name="pack",
    )(pairing, block_ids.reshape(1, count), rows, centroids)


def fill_wide(wide_ref, tiles_ref):
    tile_rows, width = tiles_ref.shape
    wide_ref[:tile_rows] = tiles_ref[...]
    wide_ref[tile_rows:] = jnp.where(iota((FLAG_ROWS, width), 1) == 0, 1.0, 0.0).astype(BF16)


def score(inner, wide_ref, x_ref, aff_ref, start=0):
    tile_rows, block = aff_ref.shape[1:]
    width = wide_ref.shape[1]
    count = inner // x_ref.shape[2]
    for n in range(block // inner):
        lanes = slice(n * inner, (n + 1) * inner)
        x = x_ref[pl.ds(start + n * count, count)].reshape(inner, width)
        scores = dot(wide_ref[...], x, ((1,), (1,)))
        aff = jnp.exp2((KAPPA * math.log2(math.e)) * scores[:tile_rows])
        aff_ref[0, :, lanes] = aff.astype(BF16)
        yield lanes, jnp.sum(aff, axis=0, keepdims=True), scores[tile_rows:][:1]


def spread(total, lanes, capacity, out_ref):
    for v in range(total.shape[1] // 128):
        piece = total[:, v * 128 : (v + 1) * 128]
        for k in range(128 // capacity):
            source = (lanes.start + v * 128) // capacity + k
            out_ref[source, :, -128:] = pltpu.roll(piece, (128 - k * capacity) % 128, 1)


def first_kernel(inner, tiles_ref, x_ref, aff_ref, total_ref, flag_ref, wide_ref):
    @pl.when((pl.program_id(0) == 0) & (pl.program_id(1) == 0))
    def _():
        fill_wide(wide_ref, tiles_ref)

    for lanes, total, flag in score(inner, wide_ref, x_ref, aff_ref):
        total_ref[0, :, lanes] = total
        flag_ref[0, :, lanes] = flag


def own_kernel(inner, tiles_ref, x_ref, aff_ref, total_ref, spread_ref, wide_ref):
    for lanes, total, _ in score(inner, tiles_ref, x_ref, aff_ref):
        total_ref[0, :, lanes] = total
        spread(total, lanes, x_ref.shape[2], spread_ref)


def other_kernel(
    inner,
    tiles_ref,
    x_ref,
    own_total_ref,
    own_flag_ref,
    own_spread_ref,
    _,
    aff_ref,
    total_ref,
    flag_ref,
    spread_ref,
    wide_ref,
):
    @pl.when(pl.program_id(1) == 0)
    def _():
        fill_wide(wide_ref, tiles_ref)

    total_ref[0] = own_total_ref[0]
    flag_ref[0] = own_flag_ref[0]
    spread_ref[:, :, :128] = own_spread_ref[...]
    start = pl.program_id(1) * (aff_ref.shape[2] // x_ref.shape[2])
    for lanes, total, flag in score(inner, wide_ref, x_ref, aff_ref, start):
        total_ref[1, :, lanes] = total
        flag_ref[1, :, lanes] = flag
        spread(total, lanes, x_ref.shape[2], spread_ref)


def affinity(kernel, tiles, x, kinds, extra, block, inner):
    tile_rows, width = tiles.shape
    sources, _, capacity, _ = x.shape
    slots = sources * capacity
    count = block // capacity
    row_shape = jax.ShapeDtypeStruct((kinds, 1, slots), F32)
    row_spec = pl.BlockSpec((1, 1, block), lambda c, i: (c, 0, i))
    both_shape = jax.ShapeDtypeStruct((2, 1, slots), F32)
    both_spec = pl.BlockSpec((2, 1, block), lambda c, i: (0, 0, i))
    spread_spec = pl.BlockSpec((count, 1, 128), lambda c, i: (i, 0, 0))
    at = 1 if kernel is other_kernel else 0
    out_specs = [pl.BlockSpec((1, tile_rows, block), lambda c, i: (c + at, 0, i))]
    out_shape = [jax.ShapeDtypeStruct((2, tile_rows, slots), BF16)]
    extra_specs = []
    x_spec = pl.BlockSpec((count, 1, capacity, width), lambda c, i: (i, c, 0, 0))
    if kernel is first_kernel:
        out_specs += [row_spec, row_spec]
        out_shape += [row_shape, row_shape]
    elif kernel is own_kernel:
        out_specs += [row_spec, spread_spec]
        out_shape += [row_shape, jax.ShapeDtypeStruct((sources, 1, 128), F32)]
    else:
        x_spec = pl.BlockSpec(memory_space=VMEM)
        extra_specs = [row_spec, row_spec, spread_spec, pl.BlockSpec(memory_space=pl.ANY)]
        out_specs += [both_spec, both_spec, pl.BlockSpec((count, 1, 256), lambda c, i: (i, 0, 0))]
        out_shape += [both_shape, both_shape, jax.ShapeDtypeStruct((sources, 1, 256), F32)]
    return pl.pallas_call(
        functools.partial(kernel, inner),
        grid=(kinds, slots // block),
        in_specs=[
            pl.BlockSpec((tile_rows, width), lambda c, i: (0, 0)),
            x_spec,
        ]
        + extra_specs,
        out_specs=out_specs,
        out_shape=out_shape,
        input_output_aliases={5: 0} if at else {},
        scratch_shapes=[VMEM((tile_rows + FLAG_ROWS, width), BF16)],
        cost_estimate=pl.CostEstimate(
            flops=2 * kinds * slots * tile_rows * width,
            bytes_accessed=kinds * (8 << 20),
            transcendentals=kinds * slots * tile_rows,
        ),
        name="affinity",
    )(tiles, x, *extra)


def add_block(aff_ref, x, total_ref, swapped_ref, flag_ref, acc_ref, count_ref):
    block = aff_ref.shape[2]
    width = acc_ref.shape[1]
    total = total_ref[0] + swapped_ref[0]
    inverse = jnp.where(flag_ref[0] < LIMIT, 1.0 / total, 0.0)
    weights = aff_ref[0].astype(F32) * inverse
    part = weights[:, :128]
    for n in range(1, block // 128):
        part = part + weights[:, n * 128 : (n + 1) * 128]
    count_ref[...] += part
    acc_ref[...] += dot(weights.astype(BF16), x.reshape(-1, width), ((1,), (0,)))


def sums_kernel(last, tiles_ref, total_ref, swapped_ref, flag_ref, aff_ref, *rest):
    *xs, out_ref, acc_ref, count_ref = rest
    c, i = pl.program_id(0), pl.program_id(1)
    width = tiles_ref.shape[1]

    @pl.when((c == 0) & (i == 0))
    def _():
        acc_ref[...] = jnp.zeros_like(acc_ref)
        count_ref[...] = jnp.zeros_like(count_ref)

    for kind, x_ref in enumerate(xs):

        @pl.when((c == kind) | (len(xs) == 1))
        def _():
            per = aff_ref.shape[2] // x_ref.shape[2]
            x = x_ref[pl.ds(i * per, per)] if kind else x_ref[...]
            add_block(aff_ref, x, total_ref, swapped_ref, flag_ref, acc_ref, count_ref)

    @pl.when((c == pl.num_programs(0) - 1) & (i == pl.num_programs(1) - 1))
    def _():
        counts = jnp.sum(count_ref[...], axis=1, keepdims=True)
        centers = (
            math.sqrt(width) * (acc_ref[...] + tiles_ref[...].astype(F32)) / (counts + 1.0)
        )
        out_ref[...] = centers if last else unit_vectors(centers)


def sums(tiles, total, swapped, flag, aff, xs, last, block):
    tile_rows, width = tiles.shape
    sources, _, capacity, _ = xs[0].shape
    slots = sources * capacity
    steps = slots // block
    row_spec = pl.BlockSpec((1, 1, block), lambda c, i: (c, 0, i))
    x_shape = (block // capacity, 1, capacity, width)
    if len(xs) == 1:
        x_specs = [pl.BlockSpec(x_shape, lambda c, i: (i, c, 0, 0))]
    else:
        x_specs = [
            pl.BlockSpec(x_shape, lambda c, i: (jnp.where(c == 0, i, steps - 1), 0, 0, 0)),
            pl.BlockSpec(memory_space=VMEM),
        ]
    return pl.pallas_call(
        functools.partial(sums_kernel, last),
        grid=(2, steps),
        in_specs=[
            pl.BlockSpec((tile_rows, width), lambda c, i: (0, 0)),
            row_spec,
            pl.BlockSpec((1, 1, block), lambda c, i: (1 - c, 0, i)),
            row_spec,
            pl.BlockSpec((1, tile_rows, block), lambda c, i: (c, 0, i)),
        ]
        + x_specs,
        out_specs=pl.BlockSpec((tile_rows, width), lambda c, i: (0, 0)),
        out_shape=jax.ShapeDtypeStruct((tile_rows, width), F32 if last else BF16),
        scratch_shapes=[VMEM((tile_rows, width), F32), VMEM((tile_rows, 128), F32)],
        cost_estimate=pl.CostEstimate(
            flops=4 * slots * tile_rows * width, bytes_accessed=16 << 20, transcendentals=0
        ),
        name="sums",
    )(tiles, total, swapped, flag, aff, *xs)


def thirds(values):
    high = values.astype(BF16)
    rest = values - high.astype(F32)
    middle = rest.astype(BF16)
    low = (rest - middle.astype(F32)).astype(BF16)
    return jnp.concatenate([high, middle, low], axis=0)


def energy_kernel(capacity, columns, pair_ref, back_ref, marks_ref, place_ref, out_ref):
    devices = back_ref.shape[0]
    across = jnp.where(
        jnp.bitwise_xor(iota((devices, devices), 0), pair_ref[PASSES - 1])
        == iota((devices, devices), 1),
        1.0,
        0.0,
    )
    own = thirds(back_ref[:, 0, :128].T[:capacity])
    other = thirds(back_ref[:, 0, 128:].T[:capacity])
    other = dot(other, across.astype(BF16), ((1,), (0,))).astype(BF16)
    found = dot(jnp.concatenate([own, other], axis=0), marks_ref[...], ((1,), (0,)))
    sums = found[:capacity]
    for n in range(1, 6):
        sums = sums + found[n * capacity : (n + 1) * capacity]
    mine = jnp.where(iota(sums.shape, 0) == place_ref[...], sums, 0.0)
    out_ref[...] = jnp.log(jnp.sum(mine, axis=0, keepdims=True) / columns)


def energies(pairing, back, marks, place, capacity, columns):
    whole = pl.BlockSpec(memory_space=VMEM)
    return pl.pallas_call(
        functools.partial(energy_kernel, capacity, columns),
        in_specs=[pl.BlockSpec(memory_space=pltpu.SMEM), whole, whole, whole],
        out_specs=whole,
        out_shape=jax.ShapeDtypeStruct(place.shape, F32),
        name="energies",
    )(pairing, back, marks, place)


def partner_swap(value, mask, width):
    def branch(apart):
        if apart == 0:
            return lambda current: current
        return lambda current: lax.ppermute(current, "blk", [(i, i ^ apart) for i in range(width)])

    return lax.switch(mask, [branch(apart) for apart in range(width)], value)


def on_device(rows, block_ids, centroids, pairing):
    groups = lax.axis_size("dp")
    members = lax.axis_size("blk")
    devices = groups * members
    rows_dev, width = rows.shape
    tile_rows = centroids.shape[0]
    capacity = 2 * rows_dev // devices
    sent, late, marks, place, tiles = pack(
        rows, block_ids, centroids, pairing, groups, members, capacity, 4
    )

    def exchanged(value, slots):
        got = lax.all_to_all(
            value.reshape(devices, -1, value.shape[-1]),
            ("dp", "blk"),
            split_axis=0,
            concat_axis=0,
            tiled=True,
        )
        return got.reshape(devices, slots, -1, value.shape[-1])

    got = exchanged(sent, 2)
    got, pairing = lax.optimization_barrier((got, pairing))
    aff, total, flag = affinity(first_kernel, tiles, got, 2, (), 1024, 512)
    swapped = partner_swap(total, pairing[0], members)
    swapped, late = lax.optimization_barrier((swapped, late))
    got_late = pltpu.with_memory_space_constraint(exchanged(late, 1), VMEM)
    tiles = sums(tiles, total, swapped, flag, aff, (got,), False, 1024)
    aff, own_total, own_spread = affinity(own_kernel, tiles, got, 1, (), 1024, 512)
    aff, total, flag, parts = affinity(
        other_kernel, tiles, got_late, 1, (own_total, flag, own_spread, aff), 1024, 512
    )
    swapped = partner_swap(total, pairing[1], members)
    swapped, parts = lax.optimization_barrier((swapped, parts))
    back = exchanged(parts, 1).reshape(devices, 1, 256)
    back = pltpu.with_memory_space_constraint(back, VMEM)
    centers = sums(tiles, total, swapped, flag, aff, (got, got_late), True, 1024)
    energy = energies(pairing, back, marks, place, capacity, 2.0 * tile_rows)
    return (centers, energy.reshape(rows_dev))


def solution(mesh):
    in_specs = (P(("dp", "blk"), None), P(("dp", "blk"), None), P(("dp", "blk"), None), P())
    out_specs = (P(("dp", "blk"), None), P(("dp", "blk")))
    return jax.shard_map(
        on_device, mesh=mesh, in_specs=in_specs, out_specs=out_specs, check_vma=False
    )
```

```python
import functools
import math

import jax
import jax.numpy as jnp
from jax import lax
from jax.experimental import pallas as pl
from jax.experimental.pallas import tpu as pltpu
from jax.sharding import PartitionSpec as P

PASSES = 2
KAPPA = 64.0
ABSENT = 1.25
LIMIT = 1.125
EPS = 1e-06
FLAG_ROWS = 16
VMEM = pltpu.VMEM
F32 = jnp.float32
BF16 = jnp.bfloat16


def unit_vectors(values):
    wide = values.astype(F32)
    scale = lax.rsqrt(jnp.mean(wide * wide, axis=-1, keepdims=True) + EPS) * values.shape[-1] ** (
        -0.5
    )
    return (wide * scale).astype(BF16)


def iota(shape, axis):
    return lax.broadcasted_iota(jnp.int32, shape, axis)


def dot(left, right, dims, precision=None):
    return lax.dot_general(
        left, right, (dims, ((), ())), preferred_element_type=F32, precision=precision
    )


def pack_kernel(
    capacity,
    pair_ref,
    ids_ref,
    rows_ref,
    tiles_ref,
    out_ref,
    late_ref,
    marks_ref,
    place_ref,
    units_ref,
    unit_ref,
    spot_ref,
    held_ref,
    y_ref,
):
    g = pl.program_id(0)
    rows = rows_ref.shape[0]
    devices = marks_ref.shape[0]
    slots = y_ref.shape[0]
    groups, members = out_ref.shape[:2]

    @pl.when(g == 0)
    def _():
        unit_ref[...] = unit_vectors(rows_ref[...])
        marks = jnp.where(ids_ref[...] == iota((devices, rows), 0), 1.0, 0.0)
        marks_ref[...] = marks.astype(BF16)
        pieces = [marks[:, n : n + 128] for n in range(0, rows, 128)]
        before = jnp.where(iota((128, 128), 0) < iota((128, 128), 1), 1.0, 0.0).astype(BF16)
        seen = dot(jnp.concatenate(pieces, axis=0).astype(BF16), before, ((1,), (0,)))
        whose = iota((devices, 128), 0).astype(F32)
        passed = jnp.zeros((devices, 1), F32)
        for n, piece in enumerate(pieces):
            lanes = slice(n * 128, (n + 1) * 128)
            here = seen[n * devices : (n + 1) * devices] + passed
            place = jnp.sum(here * piece, axis=0, keepdims=True)
            owner = jnp.sum(whose * piece, axis=0, keepdims=True)
            place_ref[:, lanes] = place.astype(jnp.int32)
            spot_ref[:, lanes] = (owner * capacity + place).astype(jnp.int32)
            passed = passed + jnp.sum(piece, axis=1, keepdims=True)
        held_ref[...] = jnp.broadcast_to(passed, (devices, 128)).astype(BF16)

    units_ref[...] = unit_vectors(tiles_ref[...])
    here = slots // capacity
    named = marks_ref[pl.ds(pl.multiple_of(g * here, here), here), :]
    level = jnp.where(iota((capacity, rows), 0) == place_ref[...], 1.0, 0.0).astype(BF16)
    chosen = jnp.concatenate([level * named[n : n + 1] for n in range(here)], axis=0)
    whose = (iota((slots, devices), 0) + g * slots) // capacity
    mine = jnp.where(whose == iota((slots, devices), 1), 1.0, 0.0).astype(BF16)
    held = dot(mine, held_ref[...], ((1,), (0,)))
    lacks = (iota((slots, 128), 0) % capacity).astype(F32) >= held
    y = dot(chosen, unit_ref[...], ((1,), (0,)))
    mark = jnp.where(lacks & (iota((slots, 128), 1) == 0), ABSENT, 0.0)
    y_ref[...] = y.astype(BF16)
    y_ref[:, :128] = (y[:, :128] + mark).astype(BF16)
    for h in range(groups):
        base = h * members * capacity
        for k in range(members):
            out_ref[h, k, 0] = y_ref[base + k * capacity : base + (k + 1) * capacity, :]
            for p in range(PASSES):
                start = base + jnp.bitwise_xor(pair_ref[p], k) * capacity
                chunk = y_ref[pl.ds(pl.multiple_of(start, capacity), capacity), :]
                if p == 0:
                    out_ref[h, k, 1] = chunk
                else:
                    late_ref[h, k] = chunk


def pack(rows, block_ids, centroids, pairing, groups, members, capacity, steps):
    count, width = rows.shape
    tile_spec = pl.BlockSpec((centroids.shape[0] // steps, width), lambda g: (g, 0))
    devices = groups * members
    return pl.pallas_call(
        functools.partial(pack_kernel, capacity),
        grid=(steps,),
        in_specs=[
            pl.BlockSpec(memory_space=pltpu.SMEM),
            pl.BlockSpec((1, count), lambda g: (0, 0)),
            pl.BlockSpec((count, width), lambda g: (0, 0)),
            tile_spec,
        ],
        out_specs=[
            pl.BlockSpec(
                (groups // steps, members, 2, capacity, width), lambda g: (g, 0, 0, 0, 0)
            ),
            pl.BlockSpec((groups // steps, members, capacity, width), lambda g: (g, 0, 0, 0)),
            pl.BlockSpec((devices, count), lambda g: (0, 0)),
            pl.BlockSpec((1, count), lambda g: (0, 0)),
            tile_spec,
        ],
        out_shape=[
            jax.ShapeDtypeStruct((groups, members, 2, capacity, width), BF16),
            jax.ShapeDtypeStruct((groups, members, capacity, width), BF16),
            jax.ShapeDtypeStruct((devices, count), BF16),
            jax.ShapeDtypeStruct((1, count), jnp.int32),
            jax.ShapeDtypeStruct(centroids.shape, BF16),
        ],
        scratch_shapes=[
            VMEM((count, width), BF16),
            VMEM((1, count), jnp.int32),
            VMEM((devices, 128), BF16),
            VMEM((devices * capacity // steps, width), BF16),
        ],
        cost_estimate=pl.CostEstimate(
            flops=4 * count * count * width, bytes_accessed=20 << 20, transcendentals=0
        ),
        name="pack",
    )(pairing, block_ids.reshape(1, count), rows, centroids)


def fill_wide(wide_ref, tiles_ref):
    tile_rows, width = tiles_ref.shape
    wide_ref[:tile_rows] = tiles_ref[...]
    wide_ref[tile_rows:] = jnp.where(iota((FLAG_ROWS, width), 1) == 0, 1.0, 0.0).astype(BF16)


def score(inner, wide_ref, x_ref, aff_ref, start=0):
    tile_rows, block = aff_ref.shape[1:]
    width = wide_ref.shape[1]
    count = inner // x_ref.shape[2]
    for n in range(block // inner):
        lanes = slice(n * inner, (n + 1) * inner)
        x = x_ref[pl.ds(start + n * count, count)].reshape(inner, width)
        scores = dot(wide_ref[...], x, ((1,), (1,)))
        aff = jnp.exp2((KAPPA * math.log2(math.e)) * scores[:tile_rows])
        aff_ref[0, :, lanes] = aff.astype(BF16)
        yield lanes, jnp.sum(aff, axis=0, keepdims=True), scores[tile_rows:][:1]


def spread(total, lanes, capacity, out_ref):
    for v in range(total.shape[1] // 128):
        piece = total[:, v * 128 : (v + 1) * 128]
        for k in range(128 // capacity):
            source = (lanes.start + v * 128) // capacity + k
            out_ref[source, :, -128:] = pltpu.roll(piece, (128 - k * capacity) % 128, 1)


def first_kernel(inner, tiles_ref, x_ref, aff_ref, total_ref, flag_ref, wide_ref):
    @pl.when((pl.program_id(0) == 0) & (pl.program_id(1) == 0))
    def _():
        fill_wide(wide_ref, tiles_ref)

    for lanes, total, flag in score(inner, wide_ref, x_ref, aff_ref):
        total_ref[0, :, lanes] = total
        flag_ref[0, :, lanes] = flag


def own_kernel(inner, tiles_ref, x_ref, aff_ref, total_ref, spread_ref, wide_ref):
    for lanes, total, _ in score(inner, tiles_ref, x_ref, aff_ref):
        total_ref[0, :, lanes] = total
        spread(total, lanes, x_ref.shape[2], spread_ref)


def other_kernel(
    inner,
    tiles_ref,
    x_ref,
    own_total_ref,
    own_flag_ref,
    own_spread_ref,
    _,
    aff_ref,
    total_ref,
    flag_ref,
    spread_ref,
    wide_ref,
):
    @pl.when(pl.program_id(1) == 0)
    def _():
        fill_wide(wide_ref, tiles_ref)

    total_ref[0] = own_total_ref[0]
    flag_ref[0] = own_flag_ref[0]
    spread_ref[:, :, :128] = own_spread_ref[...]
    start = pl.program_id(1) * (aff_ref.shape[2] // x_ref.shape[2])
    for lanes, total, flag in score(inner, wide_ref, x_ref, aff_ref, start):
        total_ref[1, :, lanes] = total
        flag_ref[1, :, lanes] = flag
        spread(total, lanes, x_ref.shape[2], spread_ref)


def affinity(kernel, tiles, x, kinds, extra, block, inner):
    tile_rows, width = tiles.shape
    sources, _, capacity, _ = x.shape
    slots = sources * capacity
    count = block // capacity
    row_shape = jax.ShapeDtypeStruct((kinds, 1, slots), F32)
    row_spec = pl.BlockSpec((1, 1, block), lambda c, i: (c, 0, i))
    both_shape = jax.ShapeDtypeStruct((2, 1, slots), F32)
    both_spec = pl.BlockSpec((2, 1, block), lambda c, i: (0, 0, i))
    spread_spec = pl.BlockSpec((count, 1, 128), lambda c, i: (i, 0, 0))
    at = 1 if kernel is other_kernel else 0
    out_specs = [pl.BlockSpec((1, tile_rows, block), lambda c, i: (c + at, 0, i))]
    out_shape = [jax.ShapeDtypeStruct((2, tile_rows, slots), BF16)]
    extra_specs = []
    x_spec = pl.BlockSpec((count, 1, capacity, width), lambda c, i: (i, c, 0, 0))
    if kernel is first_kernel:
        out_specs += [row_spec, row_spec]
        out_shape += [row_shape, row_shape]
    elif kernel is own_kernel:
        out_specs += [row_spec, spread_spec]
        out_shape += [row_shape, jax.ShapeDtypeStruct((sources, 1, 128), F32)]
    else:
        x_spec = pl.BlockSpec(memory_space=VMEM)
        extra_specs = [row_spec, row_spec, spread_spec, pl.BlockSpec(memory_space=pl.ANY)]
        out_specs += [both_spec, both_spec, pl.BlockSpec((count, 1, 256), lambda c, i: (i, 0, 0))]
        out_shape += [both_shape, both_shape, jax.ShapeDtypeStruct((sources, 1, 256), F32)]
    return pl.pallas_call(
        functools.partial(kernel, inner),
        grid=(kinds, slots // block),
        in_specs=[
            pl.BlockSpec((tile_rows, width), lambda c, i: (0, 0)),
            x_spec,
        ]
        + extra_specs,
        out_specs=out_specs,
        out_shape=out_shape,
        input_output_aliases={5: 0} if at else {},
        scratch_shapes=[VMEM((tile_rows + FLAG_ROWS, width), BF16)],
        cost_estimate=pl.CostEstimate(
            flops=2 * kinds * slots * tile_rows * width,
            bytes_accessed=kinds * (8 << 20),
            transcendentals=kinds * slots * tile_rows,
        ),
        name="affinity",
    )(tiles, x, *extra)


def add_block(aff_ref, x, total_ref, swapped_ref, flag_ref, acc_ref, count_ref):
    block = aff_ref.shape[2]
    width = acc_ref.shape[1]
    total = total_ref[0] + swapped_ref[0]
    inverse = jnp.where(flag_ref[0] < LIMIT, 1.0 / total, 0.0)
    weights = aff_ref[0].astype(F32) * inverse
    part = weights[:, :128]
    for n in range(1, block // 128):
        part = part + weights[:, n * 128 : (n + 1) * 128]
    count_ref[...] += part
    acc_ref[...] += dot(weights.astype(BF16), x.reshape(-1, width), ((1,), (0,)))


def sums_kernel(last, tiles_ref, total_ref, swapped_ref, flag_ref, aff_ref, *rest):
    *xs, out_ref, acc_ref, count_ref, sems = rest
    c, i = pl.program_id(0), pl.program_id(1)
    width = tiles_ref.shape[1]

    @pl.when((c == 0) & (i == 0))
    def _():
        acc_ref[...] = jnp.zeros_like(acc_ref)
        count_ref[...] = jnp.zeros_like(count_ref)

    for kind, x_ref in enumerate(xs):

        @pl.when((c == kind) | (len(xs) == 1))
        def _():
            per = aff_ref.shape[2] // x_ref.shape[2]
            x = x_ref[pl.ds(i * per, per)] if kind else x_ref[...]
            add_block(aff_ref, x, total_ref, swapped_ref, flag_ref, acc_ref, count_ref)

    @pl.when((c == pl.num_programs(0) - 1) & (i == pl.num_programs(1) - 1))
    def _():
        per = tiles_ref.shape[0] // sems.shape[0]
        copies = []
        for n in range(sems.shape[0]):
            part = pl.ds(n * per, per)
            counts = jnp.sum(count_ref[part], axis=1, keepdims=True)
            centers = (
                math.sqrt(width) * (acc_ref[part] + tiles_ref[part].astype(F32)) / (counts + 1.0)
            )
            if not last:
                out_ref[part] = unit_vectors(centers)
                continue
            acc_ref[part] = centers
            copy = pltpu.make_async_copy(acc_ref.at[part], out_ref.at[part], sems.at[n])
            copy.start()
            copies.append(copy)
        for copy in copies:
            copy.wait()


def sums(tiles, total, swapped, flag, aff, xs, last, block):
    tile_rows, width = tiles.shape
    sources, _, capacity, _ = xs[0].shape
    slots = sources * capacity
    steps = slots // block
    row_spec = pl.BlockSpec((1, 1, block), lambda c, i: (c, 0, i))
    x_shape = (block // capacity, 1, capacity, width)
    if len(xs) == 1:
        x_specs = [pl.BlockSpec(x_shape, lambda c, i: (i, c, 0, 0))]
    else:
        x_specs = [
            pl.BlockSpec(x_shape, lambda c, i: (jnp.where(c == 0, i, steps - 1), 0, 0, 0)),
            pl.BlockSpec(memory_space=VMEM),
        ]
    return pl.pallas_call(
        functools.partial(sums_kernel, last),
        grid=(2, steps),
        in_specs=[
            pl.BlockSpec((tile_rows, width), lambda c, i: (0, 0)),
            row_spec,
            pl.BlockSpec((1, 1, block), lambda c, i: (1 - c, 0, i)),
            row_spec,
            pl.BlockSpec((1, tile_rows, block), lambda c, i: (c, 0, i)),
        ]
        + x_specs,
        out_specs=pl.BlockSpec(memory_space=pl.ANY)
        if last
        else pl.BlockSpec((tile_rows, width), lambda c, i: (0, 0)),
        out_shape=jax.ShapeDtypeStruct((tile_rows, width), F32 if last else BF16),
        scratch_shapes=[
            VMEM((tile_rows, width), F32),
            VMEM((tile_rows, 128), F32),
            pltpu.SemaphoreType.DMA((4,)),
        ],
        cost_estimate=pl.CostEstimate(
            flops=4 * slots * tile_rows * width, bytes_accessed=16 << 20, transcendentals=0
        ),
        name="sums",
    )(tiles, total, swapped, flag, aff, *xs)


def thirds(values):
    high = values.astype(BF16)
    rest = values - high.astype(F32)
    middle = rest.astype(BF16)
    low = (rest - middle.astype(F32)).astype(BF16)
    return jnp.concatenate([high, middle, low], axis=0)


def energy_kernel(capacity, columns, pair_ref, back_ref, marks_ref, place_ref, out_ref):
    devices = back_ref.shape[0]
    across = jnp.where(
        jnp.bitwise_xor(iota((devices, devices), 0), pair_ref[PASSES - 1])
        == iota((devices, devices), 1),
        1.0,
        0.0,
    )
    own = thirds(back_ref[:, 0, :128].T[:capacity])
    other = thirds(back_ref[:, 0, 128:].T[:capacity])
    other = dot(other, across.astype(BF16), ((1,), (0,))).astype(BF16)
    found = dot(jnp.concatenate([own, other], axis=0), marks_ref[...], ((1,), (0,)))
    sums = found[:capacity]
    for n in range(1, 6):
        sums = sums + found[n * capacity : (n + 1) * capacity]
    mine = jnp.where(iota(sums.shape, 0) == place_ref[...], sums, 0.0)
    out_ref[...] = jnp.log(jnp.sum(mine, axis=0, keepdims=True) / columns)


def energies(pairing, back, marks, place, capacity, columns):
    whole = pl.BlockSpec(memory_space=VMEM)
    return pl.pallas_call(
        functools.partial(energy_kernel, capacity, columns),
        in_specs=[pl.BlockSpec(memory_space=pltpu.SMEM), whole, whole, whole],
        out_specs=whole,
        out_shape=jax.ShapeDtypeStruct(place.shape, F32),
        name="energies",
    )(pairing, back, marks, place)


def partner_swap(value, mask, width):
    def branch(apart):
        if apart == 0:
            return lambda current: current
        return lambda current: lax.ppermute(current, "blk", [(i, i ^ apart) for i in range(width)])

    return lax.switch(mask, [branch(apart) for apart in range(width)], value)


def on_device(rows, block_ids, centroids, pairing):
    groups = lax.axis_size("dp")
    members = lax.axis_size("blk")
    devices = groups * members
    rows_dev, width = rows.shape
    tile_rows = centroids.shape[0]
    capacity = 2 * rows_dev // devices
    sent, late, marks, place, tiles = pack(
        rows, block_ids, centroids, pairing, groups, members, capacity, 2
    )

    def exchanged(value, slots):
        got = lax.all_to_all(
            value.reshape(devices, -1, value.shape[-1]),
            ("dp", "blk"),
            split_axis=0,
            concat_axis=0,
            tiled=True,
        )
        return got.reshape(devices, slots, -1, value.shape[-1])

    got = exchanged(sent, 2)
    got, pairing = lax.optimization_barrier((got, pairing))
    aff, total, flag = affinity(first_kernel, tiles, got, 2, (), 1024, 512)
    swapped = partner_swap(total, pairing[0], members)
    swapped, late = lax.optimization_barrier((swapped, late))
    got_late = pltpu.with_memory_space_constraint(exchanged(late, 1), VMEM)
    tiles = sums(tiles, total, swapped, flag, aff, (got,), False, 1024)
    aff, own_total, own_spread = affinity(own_kernel, tiles, got, 1, (), 1024, 512)
    aff, total, flag, parts = affinity(
        other_kernel, tiles, got_late, 1, (own_total, flag, own_spread, aff), 1024, 512
    )
    swapped = partner_swap(total, pairing[1], members)
    swapped, parts = lax.optimization_barrier((swapped, parts))
    back = exchanged(parts, 1).reshape(devices, 1, 256)
    back = pltpu.with_memory_space_constraint(back, VMEM)
    centers = sums(tiles, total, swapped, flag, aff, (got, got_late), True, 1024)
    energy = energies(pairing, back, marks, place, capacity, 2.0 * tile_rows)
    return (centers, energy.reshape(rows_dev))


def solution(mesh):
    in_specs = (P(("dp", "blk"), None), P(("dp", "blk"), None), P(("dp", "blk"), None), P())
    out_specs = (P(("dp", "blk"), None), P(("dp", "blk")))
    return jax.shard_map(
        on_device, mesh=mesh, in_specs=in_specs, out_specs=out_specs, check_vma=False
    )
```

```python
import functools
import math

import jax
import jax.numpy as jnp
from jax import lax
from jax.experimental import pallas as pl
from jax.experimental.pallas import tpu as pltpu
from jax.sharding import PartitionSpec as P

PASSES = 2
KAPPA = 64.0
ABSENT = 1.25
LIMIT = 1.125
EPS = 1e-06
FLAG_ROWS = 16
VMEM = pltpu.VMEM
F32 = jnp.float32
BF16 = jnp.bfloat16


def unit_vectors(values):
    wide = values.astype(F32)
    scale = lax.rsqrt(jnp.mean(wide * wide, axis=-1, keepdims=True) + EPS) * values.shape[-1] ** (
        -0.5
    )
    return (wide * scale).astype(BF16)


def iota(shape, axis):
    return lax.broadcasted_iota(jnp.int32, shape, axis)


def dot(left, right, dims, precision=None):
    return lax.dot_general(
        left, right, (dims, ((), ())), preferred_element_type=F32, precision=precision
    )


def pack_kernel(
    capacity,
    pair_ref,
    ids_ref,
    rows_ref,
    tiles_ref,
    out_ref,
    late_ref,
    marks_ref,
    place_ref,
    units_ref,
    unit_ref,
    spot_ref,
    held_ref,
    y_ref,
):
    g = pl.program_id(0)
    rows = rows_ref.shape[0]
    devices = marks_ref.shape[0]
    slots = y_ref.shape[0]
    groups, members = out_ref.shape[:2]

    @pl.when(g == 0)
    def _():
        unit_ref[...] = unit_vectors(rows_ref[...])
        marks = jnp.where(ids_ref[...] == iota((devices, rows), 0), 1.0, 0.0)
        marks_ref[...] = marks.astype(BF16)
        pieces = [marks[:, n : n + 128] for n in range(0, rows, 128)]
        before = jnp.where(iota((128, 128), 0) < iota((128, 128), 1), 1.0, 0.0).astype(BF16)
        seen = dot(jnp.concatenate(pieces, axis=0).astype(BF16), before, ((1,), (0,)))
        whose = iota((devices, 128), 0).astype(F32)
        passed = jnp.zeros((devices, 1), F32)
        for n, piece in enumerate(pieces):
            lanes = slice(n * 128, (n + 1) * 128)
            here = seen[n * devices : (n + 1) * devices] + passed
            place = jnp.sum(here * piece, axis=0, keepdims=True)
            owner = jnp.sum(whose * piece, axis=0, keepdims=True)
            place_ref[:, lanes] = place.astype(jnp.int32)
            spot_ref[:, lanes] = (owner * capacity + place).astype(jnp.int32)
            passed = passed + jnp.sum(piece, axis=1, keepdims=True)
        held_ref[...] = jnp.broadcast_to(passed, (devices, 128)).astype(BF16)

    units_ref[...] = unit_vectors(tiles_ref[...])
    here = slots // capacity
    named = marks_ref[pl.ds(pl.multiple_of(g * here, here), here), :]
    level = jnp.where(iota((capacity, rows), 0) == place_ref[...], 1.0, 0.0).astype(BF16)
    chosen = jnp.concatenate([level * named[n : n + 1] for n in range(here)], axis=0)
    whose = (iota((slots, devices), 0) + g * slots) // capacity
    mine = jnp.where(whose == iota((slots, devices), 1), 1.0, 0.0).astype(BF16)
    held = dot(mine, held_ref[...], ((1,), (0,)))
    lacks = (iota((slots, 128), 0) % capacity).astype(F32) >= held
    y = dot(chosen, unit_ref[...], ((1,), (0,)))
    mark = jnp.where(lacks & (iota((slots, 128), 1) == 0), ABSENT, 0.0)
    y_ref[...] = y.astype(BF16)
    y_ref[:, :128] = (y[:, :128] + mark).astype(BF16)
    for h in range(groups):
        base = h * members * capacity
        for k in range(members):
            out_ref[h, k, 0] = y_ref[base + k * capacity : base + (k + 1) * capacity, :]
            for p in range(PASSES):
                start = base + jnp.bitwise_xor(pair_ref[p], k) * capacity
                chunk = y_ref[pl.ds(pl.multiple_of(start, capacity), capacity), :]
                if p == 0:
                    out_ref[h, k, 1] = chunk
                else:
                    late_ref[h, k] = chunk


def pack(rows, block_ids, centroids, pairing, groups, members, capacity, steps):
    count, width = rows.shape
    tile_spec = pl.BlockSpec((centroids.shape[0] // steps, width), lambda g: (g, 0))
    devices = groups * members
    return pl.pallas_call(
        functools.partial(pack_kernel, capacity),
        grid=(steps,),
        in_specs=[
            pl.BlockSpec(memory_space=pltpu.SMEM),
            pl.BlockSpec((1, count), lambda g: (0, 0)),
            pl.BlockSpec((count, width), lambda g: (0, 0)),
            tile_spec,
        ],
        out_specs=[
            pl.BlockSpec(
                (groups // steps, members, 2, capacity, width), lambda g: (g, 0, 0, 0, 0)
            ),
            pl.BlockSpec((groups // steps, members, capacity, width), lambda g: (g, 0, 0, 0)),
            pl.BlockSpec((devices, count), lambda g: (0, 0)),
            pl.BlockSpec((1, count), lambda g: (0, 0)),
            tile_spec,
        ],
        out_shape=[
            jax.ShapeDtypeStruct((groups, members, 2, capacity, width), BF16),
            jax.ShapeDtypeStruct((groups, members, capacity, width), BF16),
            jax.ShapeDtypeStruct((devices, count), BF16),
            jax.ShapeDtypeStruct((1, count), jnp.int32),
            jax.ShapeDtypeStruct(centroids.shape, BF16),
        ],
        scratch_shapes=[
            VMEM((count, width), BF16),
            VMEM((1, count), jnp.int32),
            VMEM((devices, 128), BF16),
            VMEM((devices * capacity // steps, width), BF16),
        ],
        cost_estimate=pl.CostEstimate(
            flops=4 * count * count * width, bytes_accessed=20 << 20, transcendentals=0
        ),
        name="pack",
    )(pairing, block_ids.reshape(1, count), rows, centroids)


def fill_wide(wide_ref, tiles_ref):
    tile_rows, width = tiles_ref.shape
    wide_ref[:tile_rows] = tiles_ref[...]
    wide_ref[tile_rows:] = jnp.where(iota((FLAG_ROWS, width), 1) == 0, 1.0, 0.0).astype(BF16)


def score(inner, wide_ref, x_ref, aff_ref, start=0):
    tile_rows, block = aff_ref.shape[1:]
    width = wide_ref.shape[1]
    count = inner // x_ref.shape[2]
    for n in range(block // inner):
        lanes = slice(n * inner, (n + 1) * inner)
        x = x_ref[pl.ds(start + n * count, count)].reshape(inner, width)
        scores = dot(wide_ref[...], x, ((1,), (1,)))
        aff = jnp.exp2((KAPPA * math.log2(math.e)) * scores[:tile_rows])
        aff_ref[0, :, lanes] = aff.astype(BF16)
        yield lanes, jnp.sum(aff, axis=0, keepdims=True), scores[tile_rows:][:1]


def spread(total, lanes, capacity, out_ref):
    for v in range(total.shape[1] // 128):
        piece = total[:, v * 128 : (v + 1) * 128]
        for k in range(128 // capacity):
            source = (lanes.start + v * 128) // capacity + k
            out_ref[source, :, -128:] = pltpu.roll(piece, (128 - k * capacity) % 128, 1)


def first_kernel(inner, tiles_ref, x_ref, aff_ref, total_ref, flag_ref, wide_ref):
    @pl.when((pl.program_id(0) == 0) & (pl.program_id(1) == 0))
    def _():
        fill_wide(wide_ref, tiles_ref)

    for lanes, total, flag in score(inner, wide_ref, x_ref, aff_ref):
        total_ref[0, :, lanes] = total
        flag_ref[0, :, lanes] = flag


def own_kernel(inner, tiles_ref, x_ref, aff_ref, total_ref, spread_ref, wide_ref):
    for lanes, total, _ in score(inner, tiles_ref, x_ref, aff_ref):
        total_ref[0, :, lanes] = total
        spread(total, lanes, x_ref.shape[2], spread_ref)


def other_kernel(
    inner,
    tiles_ref,
    x_ref,
    own_total_ref,
    own_flag_ref,
    own_spread_ref,
    _,
    aff_ref,
    total_ref,
    flag_ref,
    spread_ref,
    wide_ref,
):
    @pl.when(pl.program_id(1) == 0)
    def _():
        fill_wide(wide_ref, tiles_ref)

    total_ref[0] = own_total_ref[0]
    flag_ref[0] = own_flag_ref[0]
    spread_ref[:, :, :128] = own_spread_ref[...]
    start = pl.program_id(1) * (aff_ref.shape[2] // x_ref.shape[2])
    for lanes, total, flag in score(inner, wide_ref, x_ref, aff_ref, start):
        total_ref[1, :, lanes] = total
        flag_ref[1, :, lanes] = flag
        spread(total, lanes, x_ref.shape[2], spread_ref)


def affinity(kernel, tiles, x, kinds, extra, block, inner):
    tile_rows, width = tiles.shape
    sources, _, capacity, _ = x.shape
    slots = sources * capacity
    count = block // capacity
    row_shape = jax.ShapeDtypeStruct((kinds, 1, slots), F32)
    row_spec = pl.BlockSpec((1, 1, block), lambda c, i: (c, 0, i))
    both_shape = jax.ShapeDtypeStruct((2, 1, slots), F32)
    both_spec = pl.BlockSpec((2, 1, block), lambda c, i: (0, 0, i))
    spread_spec = pl.BlockSpec((count, 1, 128), lambda c, i: (i, 0, 0))
    at = 1 if kernel is other_kernel else 0
    out_specs = [pl.BlockSpec((1, tile_rows, block), lambda c, i: (c + at, 0, i))]
    out_shape = [jax.ShapeDtypeStruct((2, tile_rows, slots), BF16)]
    extra_specs = []
    x_spec = pl.BlockSpec((count, 1, capacity, width), lambda c, i: (i, c, 0, 0))
    if kernel is first_kernel:
        out_specs += [row_spec, row_spec]
        out_shape += [row_shape, row_shape]
    elif kernel is own_kernel:
        out_specs += [row_spec, spread_spec]
        out_shape += [row_shape, jax.ShapeDtypeStruct((sources, 1, 128), F32)]
    else:
        x_spec = pl.BlockSpec(memory_space=VMEM)
        extra_specs = [row_spec, row_spec, spread_spec, pl.BlockSpec(memory_space=pl.ANY)]
        out_specs += [both_spec, both_spec, pl.BlockSpec((count, 1, 256), lambda c, i: (i, 0, 0))]
        out_shape += [both_shape, both_shape, jax.ShapeDtypeStruct((sources, 1, 256), F32)]
    return pl.pallas_call(
        functools.partial(kernel, inner),
        grid=(kinds, slots // block),
        in_specs=[
            pl.BlockSpec(memory_space=VMEM)
            if kernel is first_kernel
            else pl.BlockSpec((tile_rows, width), lambda c, i: (0, 0)),
            x_spec,
        ]
        + extra_specs,
        out_specs=out_specs,
        out_shape=out_shape,
        input_output_aliases={5: 0} if at else {},
        scratch_shapes=[VMEM((tile_rows + FLAG_ROWS, width), BF16)],
        cost_estimate=pl.CostEstimate(
            flops=2 * kinds * slots * tile_rows * width,
            bytes_accessed=kinds * (8 << 20),
            transcendentals=kinds * slots * tile_rows,
        ),
        name="affinity",
    )(tiles, x, *extra)


def add_block(aff_ref, x, total_ref, swapped_ref, flag_ref, acc_ref, count_ref):
    block = aff_ref.shape[2]
    width = acc_ref.shape[1]
    total = total_ref[0] + swapped_ref[0]
    inverse = jnp.where(flag_ref[0] < LIMIT, 1.0 / total, 0.0)
    weights = aff_ref[0].astype(F32) * inverse
    part = weights[:, :128]
    for n in range(1, block // 128):
        part = part + weights[:, n * 128 : (n + 1) * 128]
    count_ref[...] += part
    acc_ref[...] += dot(weights.astype(BF16), x.reshape(-1, width), ((1,), (0,)))


def sums_kernel(last, tiles_ref, total_ref, swapped_ref, flag_ref, aff_ref, *rest):
    *xs, out_ref, acc_ref, count_ref, sems = rest
    c, i = pl.program_id(0), pl.program_id(1)
    width = tiles_ref.shape[1]

    @pl.when((c == 0) & (i == 0))
    def _():
        acc_ref[...] = jnp.zeros_like(acc_ref)
        count_ref[...] = jnp.zeros_like(count_ref)

    for kind, x_ref in enumerate(xs):

        @pl.when((c == kind) | (len(xs) == 1))
        def _():
            per = aff_ref.shape[2] // x_ref.shape[2]
            x = x_ref[pl.ds(i * per, per)] if kind else x_ref[...]
            add_block(aff_ref, x, total_ref, swapped_ref, flag_ref, acc_ref, count_ref)

    @pl.when((c == pl.num_programs(0) - 1) & (i == pl.num_programs(1) - 1))
    def _():
        per = tiles_ref.shape[0] // sems.shape[0]
        copies = []
        for n in range(sems.shape[0]):
            part = pl.ds(n * per, per)
            counts = jnp.sum(count_ref[part], axis=1, keepdims=True)
            centers = (
                math.sqrt(width) * (acc_ref[part] + tiles_ref[part].astype(F32)) / (counts + 1.0)
            )
            if not last:
                out_ref[part] = unit_vectors(centers)
                continue
            acc_ref[part] = centers
            copy = pltpu.make_async_copy(acc_ref.at[part], out_ref.at[part], sems.at[n])
            copy.start()
            copies.append(copy)
        for copy in copies:
            copy.wait()


def sums(tiles, total, swapped, flag, aff, xs, last, block):
    tile_rows, width = tiles.shape
    sources, _, capacity, _ = xs[0].shape
    slots = sources * capacity
    steps = slots // block
    row_spec = pl.BlockSpec((1, 1, block), lambda c, i: (c, 0, i))
    x_shape = (block // capacity, 1, capacity, width)
    if len(xs) == 1:
        x_specs = [pl.BlockSpec(x_shape, lambda c, i: (i, c, 0, 0))]
    else:
        x_specs = [
            pl.BlockSpec(x_shape, lambda c, i: (jnp.where(c == 0, i, steps - 1), 0, 0, 0)),
            pl.BlockSpec(memory_space=VMEM),
        ]
    return pl.pallas_call(
        functools.partial(sums_kernel, last),
        grid=(2, steps),
        in_specs=[
            pl.BlockSpec((tile_rows, width), lambda c, i: (0, 0)),
            row_spec,
            pl.BlockSpec((1, 1, block), lambda c, i: (1 - c, 0, i)),
            row_spec,
            pl.BlockSpec((1, tile_rows, block), lambda c, i: (c, 0, i)),
        ]
        + x_specs,
        out_specs=pl.BlockSpec(memory_space=pl.ANY)
        if last
        else pl.BlockSpec((tile_rows, width), lambda c, i: (0, 0)),
        out_shape=jax.ShapeDtypeStruct((tile_rows, width), F32 if last else BF16),
        scratch_shapes=[
            VMEM((tile_rows, width), F32),
            VMEM((tile_rows, 128), F32),
            pltpu.SemaphoreType.DMA((4,)),
        ],
        cost_estimate=pl.CostEstimate(
            flops=4 * slots * tile_rows * width, bytes_accessed=16 << 20, transcendentals=0
        ),
        name="sums",
    )(tiles, total, swapped, flag, aff, *xs)


def thirds(values):
    high = values.astype(BF16)
    rest = values - high.astype(F32)
    middle = rest.astype(BF16)
    low = (rest - middle.astype(F32)).astype(BF16)
    return jnp.concatenate([high, middle, low], axis=0)


def energy_kernel(capacity, columns, pair_ref, back_ref, marks_ref, place_ref, out_ref):
    devices = back_ref.shape[0]
    across = jnp.where(
        jnp.bitwise_xor(iota((devices, devices), 0), pair_ref[PASSES - 1])
        == iota((devices, devices), 1),
        1.0,
        0.0,
    )
    own = thirds(back_ref[:, 0, :128].T[:capacity])
    other = thirds(back_ref[:, 0, 128:].T[:capacity])
    other = dot(other, across.astype(BF16), ((1,), (0,))).astype(BF16)
    found = dot(jnp.concatenate([own, other], axis=0), marks_ref[...], ((1,), (0,)))
    sums = found[:capacity]
    for n in range(1, 6):
        sums = sums + found[n * capacity : (n + 1) * capacity]
    mine = jnp.where(iota(sums.shape, 0) == place_ref[...], sums, 0.0)
    out_ref[...] = jnp.log(jnp.sum(mine, axis=0, keepdims=True) / columns)


def energies(pairing, back, marks, place, capacity, columns):
    whole = pl.BlockSpec(memory_space=VMEM)
    return pl.pallas_call(
        functools.partial(energy_kernel, capacity, columns),
        in_specs=[pl.BlockSpec(memory_space=pltpu.SMEM), whole, whole, whole],
        out_specs=whole,
        out_shape=jax.ShapeDtypeStruct(place.shape, F32),
        name="energies",
    )(pairing, back, marks, place)


def partner_swap(value, mask, width):
    def branch(apart):
        if apart == 0:
            return lambda current: current
        return lambda current: lax.ppermute(current, "blk", [(i, i ^ apart) for i in range(width)])

    return lax.switch(mask, [branch(apart) for apart in range(width)], value)


def on_device(rows, block_ids, centroids, pairing):
    groups = lax.axis_size("dp")
    members = lax.axis_size("blk")
    devices = groups * members
    rows_dev, width = rows.shape
    tile_rows = centroids.shape[0]
    capacity = 2 * rows_dev // devices
    sent, late, marks, place, tiles = pack(
        rows, block_ids, centroids, pairing, groups, members, capacity, 2
    )

    def exchanged(value, slots):
        got = lax.all_to_all(
            value.reshape(devices, -1, value.shape[-1]),
            ("dp", "blk"),
            split_axis=0,
            concat_axis=0,
            tiled=True,
        )
        return got.reshape(devices, slots, -1, value.shape[-1])

    got = exchanged(sent, 2)
    got, pairing = lax.optimization_barrier((got, pairing))
    near = pltpu.with_memory_space_constraint(tiles, VMEM)
    aff, total, flag = affinity(first_kernel, near, got, 2, (), 1024, 512)
    swapped = partner_swap(total, pairing[0], members)
    swapped, late = lax.optimization_barrier((swapped, late))
    got_late = pltpu.with_memory_space_constraint(exchanged(late, 1), VMEM)
    tiles = sums(tiles, total, swapped, flag, aff, (got,), False, 1024)
    aff, own_total, own_spread = affinity(own_kernel, tiles, got, 1, (), 1024, 512)
    aff, total, flag, parts = affinity(
        other_kernel, tiles, got_late, 1, (own_total, flag, own_spread, aff), 1024, 512
    )
    swapped = partner_swap(total, pairing[1], members)
    swapped, parts = lax.optimization_barrier((swapped, parts))
    back = exchanged(parts, 1).reshape(devices, 1, 256)
    back = pltpu.with_memory_space_constraint(back, VMEM)
    centers = sums(tiles, total, swapped, flag, aff, (got, got_late), True, 1024)
    energy = energies(pairing, back, marks, place, capacity, 2.0 * tile_rows)
    return (centers, energy.reshape(rows_dev))


def solution(mesh):
    in_specs = (P(("dp", "blk"), None), P(("dp", "blk"), None), P(("dp", "blk"), None), P())
    out_specs = (P(("dp", "blk"), None), P(("dp", "blk")))
    return jax.shard_map(
        on_device, mesh=mesh, in_specs=in_specs, out_specs=out_specs, check_vma=False
    )
```
